32 devices in a mesh: slab: 8 (over z, core), split: 4 (over y, x).
Axes of the slice: x: 2, y: 2, z: 4, core: 2. Of those that a mesh axis runs over, the one named last changes fastest.
Arguments:
- displacement: float32 [3, 64, 128, 256], P(None, 'slab', 'split'), may hold values from -0.3 to 0.3
- velocity: float32 [3, 64, 128, 256], P(None, 'slab', 'split'), may hold values from -0.6 to 0.6
- acceleration: float32 [3, 64, 128, 256], P(None, 'slab', 'split'), may hold values from -1.8 to 1.8
- bond_masks: int32 [4, 64, 128, 256], P(None, 'slab', 'split'), may hold values from 0 to 255, as said below
- proj_pos: float32 [32, 3, 128], replicated, may hold values from -0.5 to 257, as said below
- proj_vel: float32 [32, 3, 128], replicated, may hold values from -1.8 to 1.8
- proj_acc: float32 [32, 3, 128], replicated, may hold values from -1.8 to 1.8
- contact_pairs: int32 [3, 2, 512], P(None, None, ('slab', 'split')), may hold values from -1 to 31, as said below
Outputs:
- final_displacement: float32 [3, 64, 128, 256], P(None, 'slab', 'split')
- final_velocity: float32 [3, 64, 128, 256], P(None, 'slab', 'split')
- final_proj_pos: float32 [32, 3, 128], replicated
- final_proj_vel: float32 [32, 3, 128], replicated
The draws below stay inside these ranges and needn't reach their ends.
Inputs may be any that keep to these rules, and one draw needn't show every extreme that they name: `bond_masks`: bit b of word w (the value divided by 2 to the b, modulo 2) is 1 where the bond from the cell to the offset numbered 8 w + b is intact. `contact_pairs`: slots d * 16 to (d + 1) * 16 - 1 belong to device d. Row 0 names one of that device's 8 surface blocks; row 1 names a projectile block, or -1 for an empty slot. Live slots come first on every device and no pair repeats on a device within a substep. In every substep each projectile block is paired on exactly one device, one of the four devices of the 2 x 2 group of device blocks under it, and on another device than in the substep before; in every substep some device has all 16 slots live. `proj_pos`: the device blocks fall into 2 x 2 groups (slab indices 2a and 2a + 1, split indices 2b and 2b + 1). Every projectile block lies above one such group, between 0.5 and 2 cells over the top layer, and every group lies under exactly 4 projectile blocks.
All inputs are finite; a program needn't handle non-finite values.
Results may differ from the reference program's by a relative error of at most 0.0003.
Values sent between devices are 32-bit elements; how exact they have to be, the bound alone decides.
A program may use at most 128 MiB of HBM per device.

```python
import math
import jax
import jax.numpy as jnp
from jax import lax

CX = 8
CY = 32
NZ = 256
SUB = 3
SL = 4
PTS = 128
MAXH = 4
NX = 64
NY = 128
SB_DEV = 8
TPB = 4
MAXP = 16
PB = 32
N_SPLIT = 4


def quad_owners(key):
    base_key = jax.random.fold_in(key, 7)
    keys = jax.random.split(base_key, 6)
    slab_count = NX // CX
    split_count = NY // CY
    devices = slab_count * split_count
    quad_count = devices // 4
    half_split = split_count // 2
    per_quad = PB // quad_count
    quad_of = jax.random.permutation(keys[0], (jnp.arange(PB) // per_quad).astype(jnp.int32)).astype(jnp.int32)
    center = jax.random.randint(keys[1], (), 0, quad_count)
    in_center = quad_of == center
    own_start = jax.random.randint(keys[2], (PB,), 0, 4)
    own_steps = jax.random.randint(keys[3], (SUB, PB), 1, 4)
    common_start = jax.random.randint(keys[4], (), 0, 4)
    common_steps = jax.random.randint(keys[5], (SUB, 1), 1, 4)
    corner = jnp.where(in_center, common_start, own_start).astype(jnp.int32)
    step_sizes = jnp.where(in_center[None, :], common_steps, own_steps).astype(jnp.int32)
    owner_rows = []
    for substep in range(SUB):
        if substep > 0:
            corner = (corner + step_sizes[substep]) % 4
        row_index = 2 * (quad_of // half_split) + corner // 2
        column_index = 2 * (quad_of % half_split) + corner % 2
        owner_rows.append((row_index * split_count + column_index).astype(jnp.int32))
    return (quad_of, jnp.stack(owner_rows))


def draw_bond_masks(key, part):
    mask_key = jax.random.fold_in(key, 41)
    packed = jnp.zeros((4, NX, NY, NZ), jnp.int32)
    for bit_index in range(8):
        digits = jax.random.randint(jax.random.fold_in(mask_key, bit_index), (4, NX, NY, NZ), 0, 5)
        packed = packed + (digits < 4).astype(jnp.int32) * 2 ** bit_index
    return packed


def draw_contact_pairs(key, part):
    quad_of, owners = quad_owners(key)
    devices = NX // CX * (NY // CY)
    indices = jnp.arange(PB).astype(jnp.int32)
    earlier = (owners[:, None, :] == owners[:, :, None]) & (indices[None, None, :] < indices[None, :, None])
    owner_rank = jnp.sum(earlier.astype(jnp.int32), axis=2)
    step_index = jnp.broadcast_to(jnp.arange(SUB).astype(jnp.int32)[:, None], (SUB, PB))
    block_index = jnp.broadcast_to(indices[None, :], (SUB, PB))
    home_table = jnp.full((SUB, devices, MAXH), -1, jnp.int32).at[step_index, owners, owner_rank].set(block_index)
    slot_keys = jax.random.split(jax.random.fold_in(key, 13), SUB * devices * MAXH)
    target_picks = jax.vmap(lambda slot_key: jax.random.permutation(slot_key, SB_DEV)[:TPB])(slot_keys)
    targets = target_picks.reshape(SUB, devices * MAXH * TPB).astype(jnp.int32)
    chosen = jnp.broadcast_to(home_table[:, :, :, None], (SUB, devices, MAXH, TPB)).reshape(SUB, devices * MAXH * TPB)
    return jnp.stack([targets, chosen.astype(jnp.int32)], axis=1)


def draw_proj_pos(key, part):
    quad_of, owners = quad_owners(key)
    half_split = NY // CY // 2
    base_x = (quad_of // half_split * 2 * CX).astype(jnp.float32)
    base_y = (quad_of % half_split * 2 * CY).astype(jnp.float32)
    float_keys = jax.random.split(jax.random.fold_in(key, 29), 3)
    along_x = base_x[:, None] + jax.random.uniform(float_keys[0], (PB, PTS), jnp.float32, -0.5, 2 * CX - 0.5)
    along_y = base_y[:, None] + jax.random.uniform(float_keys[1], (PB, PTS), jnp.float32, -0.5, 2 * CY - 0.5)
    height = NZ - 1 + jax.random.uniform(float_keys[2], (PB, PTS), jnp.float32, 0.5, 2.0)
    return jnp.stack([along_x, along_y, height], axis=1)


def level_of(stream_key, shape, cuts, smallest, high):
    def one(dim, blocks):
        draws = jax.random.uniform(jax.random.fold_in(jax.random.fold_in(stream_key, 6), dim), (blocks,), jnp.float32, smallest / len(cuts), high / len(cuts))
        return jnp.repeat(jnp.exp(draws), shape[dim] // blocks).reshape((-1,) + (1,) * (len(shape) - dim - 1))

    factor_of = one(*cuts[0])
    for cut in cuts[1:]:
        factor_of = factor_of * one(*cut)
    return factor_of


def normal_values(stream_key, dims, width, bound, cuts=(), kind=jnp.bfloat16):
    level = level_of(stream_key, dims, cuts, -0.22, 0.18) if cuts else 1.0
    entries = jax.random.normal(stream_key, dims, jnp.float32) * width * level
    return jnp.minimum(jnp.maximum(entries, -bound), bound).astype(kind)


def setup_inputs(seed: int = 0) -> dict:
    arg_keys = jax.random.split(jax.random.key(seed), 9)
    return {
        "displacement": normal_values(arg_keys[0], (3, NX, NY, NZ), 0.05, 0.3, ((1, 8), (2, 4)), jnp.float32),
        "velocity": normal_values(arg_keys[1], (3, NX, NY, NZ), 0.1, 0.6, ((1, 8), (2, 4)), jnp.float32),
        "acceleration": normal_values(arg_keys[2], (3, NX, NY, NZ), 0.3, 1.8, ((1, 8), (2, 4)), jnp.float32),
        "bond_masks": draw_bond_masks(jax.random.fold_in(arg_keys[8], 71), 0),
        "proj_pos": draw_proj_pos(jax.random.fold_in(arg_keys[8], 71), 0),
        "proj_vel": normal_values(arg_keys[5], (PB, 3, PTS), 0.3, 1.8, (), jnp.float32),
        "proj_acc": normal_values(arg_keys[6], (PB, 3, PTS), 0.3, 1.8, (), jnp.float32),
        "contact_pairs": draw_contact_pairs(jax.random.fold_in(arg_keys[8], 71), 0),
    }


time_step = 0.25
bond_stiffness = 0.5
contact_stiffness = 0.05
contact_width = 8.0
inverse_mass = 0.5

def bond_offsets():
    listed = []
    for shift_x in (-2, -1, 0, 1, 2):
        for shift_y in (-2, -1, 0, 1, 2):
            for shift_z in (-2, -1, 0, 1, 2):
                squared = shift_x * shift_x + shift_y * shift_y + shift_z * shift_z
                if 0 < squared <= 4:
                    listed.append((shift_x, shift_y, shift_z))
    return listed

def bond_term(neighbour, displace, intact, valid_bond, offset):
    shift_x, shift_y, shift_z = offset
    length = math.sqrt(shift_x * shift_x + shift_y * shift_y + shift_z * shift_z)
    along_x = shift_x + (neighbour[0] - displace[0])
    along_y = shift_y + (neighbour[1] - displace[1])
    along_z = shift_z + (neighbour[2] - displace[2])
    squared = along_x * along_x + along_y * along_y + along_z * along_z
    stretch = (squared - length * length) / (length * (jnp.sqrt(squared) + length))
    return bond_stiffness / length * stretch * intact * valid_bond

def add_bond(bond_total, coefficient, offset):
    direction = jnp.array(offset, bond_total.dtype)
    return bond_total + direction[:, None, None, None] * coefficient[None]

def bond_forces(displace, mask_words):
    padded = jnp.pad(displace, ((0, 0), (2, 2), (2, 2), (2, 2)))
    inside_x = jnp.pad(jnp.ones((NX,), displace.dtype), 2)
    inside_y = jnp.pad(jnp.ones((NY,), displace.dtype), 2)
    inside_z = jnp.pad(jnp.ones((NZ,), displace.dtype), 2)
    bond_total = jnp.zeros_like(displace)
    for number, offset in enumerate(bond_offsets()):
        shift_x, shift_y, shift_z = offset
        neighbour = padded[:, 2 + shift_x:2 + shift_x + NX, 2 + shift_y:2 + shift_y + NY, 2 + shift_z:2 + shift_z + NZ]
        valid_bond = inside_x[2 + shift_x:2 + shift_x + NX][:, None, None] * inside_y[2 + shift_y:2 + shift_y + NY][None, :, None] * inside_z[2 + shift_z:2 + shift_z + NZ][None, None, :]
        intact = (mask_words[number // 8] // 2 ** (number % 8) % 2).astype(displace.dtype)
        bond_total = add_bond(bond_total, bond_term(neighbour, displace, intact, valid_bond, offset), offset)
    return bond_total

def contact_tile(points, particles):
    separation = points[:, :, None] - particles[:, None, :]
    squared = lax.optimization_barrier(jnp.sum(separation * separation, axis=0))
    weight = contact_stiffness * jnp.exp(-squared / contact_width)
    pulled = weight[None] * separation
    return (lax.optimization_barrier(jnp.sum(pulled, axis=2)), -lax.optimization_barrier(jnp.sum(pulled, axis=1)))

def contact_forces(displace, positions, slot_pairs):
    anchor = jnp.zeros((), jnp.int32)
    lattice = jnp.stack([jnp.broadcast_to(jnp.arange(NX).astype(displace.dtype)[:, None, None], (NX, NY, SL)), jnp.broadcast_to(jnp.arange(NY).astype(displace.dtype)[None, :, None], (NX, NY, SL)), jnp.broadcast_to((NZ - SL + jnp.arange(SL)).astype(displace.dtype)[None, None, :], (NX, NY, SL))])
    places = displace[:, :, :, NZ - SL:] + lattice

    def visit(running, slot_index):
        surface_force, particle_force = running
        device = slot_index // MAXP
        corner_x = (device // N_SPLIT * CX).astype(jnp.int32)
        corner_y = (device % N_SPLIT * CY).astype(jnp.int32)
        starts = (anchor, corner_x, corner_y, anchor)
        region = lax.dynamic_slice(places, starts, (3, CX, CY, SL)).reshape(3, SB_DEV, PTS)
        surface_block = slot_pairs[0, slot_index]
        chosen = slot_pairs[1, slot_index]
        is_live = (chosen >= 0).astype(places.dtype)
        picked = jnp.maximum(chosen, 0)
        on_points, on_particles = contact_tile(region[:, surface_block], positions[picked])
        patch_force = jnp.zeros((3, SB_DEV, PTS), places.dtype).at[:, surface_block].set(on_points * is_live)
        current = lax.dynamic_slice(surface_force, starts, (3, CX, CY, SL))
        surface_force = lax.dynamic_update_slice(surface_force, current + patch_force.reshape(3, CX, CY, SL), starts)
        particle_force = particle_force.at[picked].add(on_particles * is_live)
        return ((surface_force, particle_force), None)
    initial = (jnp.zeros_like(places), jnp.zeros_like(positions))
    finals, ignored = lax.scan(visit, initial, jnp.arange(slot_pairs.shape[1]).astype(jnp.int32))
    return finals

def reference(displacement, velocity, acceleration, bond_masks, proj_pos, proj_vel, proj_acc, contact_pairs):
    for substep in range(SUB):
        half_velocity = velocity + 0.5 * time_step * acceleration
        displacement = displacement + time_step * half_velocity
        proj_half = proj_vel + 0.5 * time_step * proj_acc
        proj_pos = proj_pos + time_step * proj_half
        forces = bond_forces(displacement, bond_masks)
        surface_force, particle_force = contact_forces(displacement, proj_pos, contact_pairs[substep])
        forces = forces + jnp.pad(surface_force, ((0, 0), (0, 0), (0, 0), (NZ - SL, 0)))
        acceleration = forces
        velocity = half_velocity + 0.5 * time_step * acceleration
        proj_acc = inverse_mass * particle_force
        proj_vel = proj_half + 0.5 * time_step * proj_acc
    return (displacement, velocity, proj_pos, proj_vel)
```

```python
import functools
import math

import jax
import jax.numpy as jnp
from jax import lax
from jax.experimental import pallas as pl
from jax.experimental.pallas import tpu as pltpu
from jax.sharding import PartitionSpec as P

SL = 4
PTS = 128
SB_DEV = 8
LANES = 128
ROWS = 16

time_step = 0.25
bond_stiffness = 0.5
contact_stiffness = 0.05
contact_width = 8.0
inverse_mass = 0.5
tiny = 1e-30
far = 1e4
MESH = pl.DeviceIdType.MESH
f32 = jnp.float32


def bond_offsets():
    listed = []
    for shift_x in (-2, -1, 0, 1, 2):
        for shift_y in (-2, -1, 0, 1, 2):
            for shift_z in (-2, -1, 0, 1, 2):
                squared = shift_x * shift_x + shift_y * shift_y + shift_z * shift_z
                if 0 < squared <= 4:
                    listed.append((shift_x, shift_y, shift_z))
    return listed


OFFSETS = bond_offsets()
NUMBER = {e: n for n, e in enumerate(OFFSETS)}
HALF = [(dx, dy, 1) for dx in (-1, 0, 1) for dy in (-1, 0, 1)] + [(0, 0, 2)] + [
    (1, 0, 0), (2, 0, 0), (0, 1, 0), (0, 2, 0), (1, 1, 0), (1, -1, 0)
]
INDEX = {e: m for m, e in enumerate(HALF)}
PAIRS = len(HALF)
CORNERS = [(-1, -1), (-1, 1), (1, -1), (1, 1)]
SIDES = [(-1, 0), (1, 0), (0, -1), (0, 1)]


def square(e):
    return e[0] * e[0] + e[1] * e[1] + e[2] * e[2]


def word_bits(test):
    words = [0, 0, 0, 0]
    for n, e in enumerate(OFFSETS):
        if test(e):
            words[n // 8] |= 1 << (n % 8)
    return words


def exact_dot(a, b):
    return lax.dot_general(
        a, b, (((1,), (0,)), ((), ())), precision=lax.Precision.HIGHEST, preferred_element_type=f32
    )


def kernel(
    dims,
    disp_hbm, vel_hbm, acc_hbm, mask_hbm, qpos_hbm, qvel_hbm, qacc_hbm, pairs_hbm,
    disp_out, vel_out, pos_out, pvel_out,
    qpos_ref, qvel_ref, qacc_ref, pairs_ref, ends,
    u_0, u_p, u_pp, dsp, vel, acc, mask_ref, valid, factors, rr, edges_y, edges_c,
    got_x, got_y, got_c, qb, psel, slot_rows, pf, pairs_s, onehot, onehot_t, penalty, place_col,
    qp, qv, part_send, part_got, fin, gathered,
    in_sem, small_sem, out_sem, end_sem, send_x, recv_x, send_y, recv_y, send_c, recv_c, send_p, recv_p, send_g, recv_g,
):
    subs, nx, ny, nz, slabs, splits, per_group, blocks = dims
    halves = nz // LANES
    tiles = ny // 8
    slots = pairs_ref.shape[2]
    per_block = slots // per_group
    top = halves - 1
    me_x = lax.axis_index("slab")
    me_y = lax.axis_index("split")
    mid_x, mid_y = nx // 2, ny // 2
    half_split = splits // 2
    groups = (slabs // 2) * half_split
    my_group = (me_x // 2) * half_split + me_y // 2
    my_x, my_y = lax.rem(me_x, 2), lax.rem(me_y, 2)
    my_id = my_x * 2 + my_y
    dt = time_step

    def exists(dx, dy):
        ok = None
        for d, me, n in ((dx, me_x, slabs), (dy, me_y, splits)):
            if d:
                cond = (me > 0) if d < 0 else (me < n - 1)
                ok = cond if ok is None else ok & cond
        return ok

    cut = nx // 2
    loads = [
        [
            pltpu.make_async_copy(
                src.at[:, i * cut : (i + 1) * cut], dst.at[:, i * cut : (i + 1) * cut], in_sem.at[a, i]
            )
            for i in range(2)
        ]
        for a, (src, dst) in enumerate(
            ((acc_hbm, acc), (vel_hbm, vel), (disp_hbm, dsp), (mask_hbm, mask_ref))
        )
    ]
    for a in range(4):
        for load in loads[a]:
            load.start()

    small = [
        pltpu.make_async_copy(src, dst, small_sem.at[i])
        for i, (src, dst) in enumerate((
            (qpos_hbm, qpos_ref), (qvel_hbm, qvel_ref), (qacc_hbm, qacc_ref), (pairs_hbm, pairs_ref)
        ))
    ]
    for load in small:
        load.start()

    barrier = pltpu.get_barrier_semaphore()

    def greet(x, y):
        pl.semaphore_signal(barrier, inc=1, device_id=(x, y), device_id_type=MESH)

    for dx, dy in SIDES + CORNERS:
        @pl.when(exists(dx, dy))
        def _():
            greet(me_x + dx, me_y + dy)

    def group_xy(g):
        return 2 * (g // half_split) + my_x, 2 * lax.rem(g, half_split) + my_y

    @pl.loop(0, groups)
    def _(g):
        @pl.when(g != my_group)
        def _():
            x, y = group_xy(g)
            greet(x, y)

    lane = lax.broadcasted_iota(jnp.int32, (8, LANES), 1)
    row8 = lax.broadcasted_iota(jnp.int32, (8, LANES), 0)
    zero_tile = jnp.zeros((8, LANES), f32)

    for ref in (u_0, u_p):
        for x in (0, 1, nx + 2, nx + 3):
            ref[:, x] = jnp.zeros(ref.shape[:1] + ref.shape[2:], f32)

        @pl.loop(2, nx + 2)
        def _(x):
            for c in range(3):
                for h in range(halves):
                    ref[c, x, h, 0:8, :] = zero_tile
                    ref[c, x, h, ny + 8 : ny + 16, :] = zero_tile

    def shifted(parts, by):
        rows = parts[0].shape[0]
        lanes = lax.broadcasted_iota(jnp.int32, (rows, LANES), 1)
        rolled = [pltpu.roll(p, (-by) % LANES, axis=1) for p in parts]
        out = []
        n = len(parts)
        for h in range(n):
            other = (h + 1) % n if by > 0 else (h - 1) % n
            edge = lanes >= LANES - by if by > 0 else lanes < -by
            out.append(jnp.where(edge, rolled[other], rolled[h]))
        return out

    def put(c, x, rows, parts, shifts=True):
        for h, p in enumerate(parts):
            u_0[c, x, h, rows, :] = p
        if shifts:
            for h, p in enumerate(shifted(parts, 1)):
                u_p[c, x, h, rows, :] = p + 1.0 if c == 2 else p

    def zs(h):
        return slice(h * LANES, (h + 1) * LANES)

    def advance(s, x, t, speeds):
        rows = slice(8 * t, 8 * t + 8)
        for c in range(3):
            parts = []
            for h in range(halves):
                half = speeds[h][c]
                vel[c, x, rows, zs(h)] = half
                moved = dsp[c, x, rows, zs(h)] + dt * half
                dsp[c, x, rows, zs(h)] = moved
                if c == 0:
                    moved = moved + (x - mid_x).astype(f32)
                elif c == 1:
                    moved = moved + (row8 + (8 * t - mid_y)).astype(f32)
                parts.append(moved)
            put(c, x + 2, slice(8 + 8 * t, 16 + 8 * t), parts)
            for h, p in enumerate(shifted(parts, 2)):
                u_pp[c, x, h, rows, :] = p + 2.0 if c == 2 else p
            for h, p in enumerate(parts):
                if t == 0:
                    edges_y[s, 0, c, x, h] = p[0:2]
                if t == tiles - 1:
                    edges_y[s, 1, c, x, h] = p[6:8]

    def near_layer(d):
        return 0 if d < 0 else nx - 1

    def copy_side(s, k, d, j):
        layer = near_layer(d) - d * j
        return pltpu.make_async_remote_copy(
            src_ref=u_0.at[:, 2 + layer, :, 8 : 8 + ny, :], dst_ref=got_x.at[s, k, j],
            send_sem=send_x.at[s, k, j], recv_sem=recv_x.at[s, k, j],
            device_id=(me_x + d, me_y), device_id_type=MESH,
        )

    def take_side(s, k, j):
        d = (-1, 1)[k]
        return pltpu.make_async_remote_copy(
            src_ref=got_x.at[s, k, j], dst_ref=got_x.at[s, k, j],
            send_sem=send_x.at[s, k, j], recv_sem=recv_x.at[s, k, j],
            device_id=(me_x + d, me_y), device_id_type=MESH,
        )

    def copy_edge(s, k, d):
        return pltpu.make_async_remote_copy(
            src_ref=edges_y.at[s, 1 - k], dst_ref=got_y.at[s, k],
            send_sem=send_y.at[s, k], recv_sem=recv_y.at[s, k],
            device_id=(me_x, me_y + d), device_id_type=MESH,
        )

    def take_edge(s, k, d):
        return pltpu.make_async_remote_copy(
            src_ref=got_y.at[s, k], dst_ref=got_y.at[s, k], send_sem=send_y.at[s, k],
            recv_sem=recv_y.at[s, k], device_id=(me_x, me_y + d), device_id_type=MESH,
        )

    def copy_corner(s, k, dx, dy):
        return pltpu.make_async_remote_copy(
            src_ref=edges_c.at[s, k], dst_ref=got_c.at[s, k], send_sem=send_c.at[s, k],
            recv_sem=recv_c.at[s, k], device_id=(me_x + dx, me_y + dy), device_id_type=MESH,
        )

    def take_corner(s, j, dx, dy):
        return pltpu.make_async_remote_copy(
            src_ref=got_c.at[s, j], dst_ref=got_c.at[s, j], send_sem=send_c.at[s, j],
            recv_sem=recv_c.at[s, j], device_id=(me_x + dx, me_y + dy), device_id_type=MESH,
        )

    partners = ((0, 1), (1, 0), (1, 1))

    def flipped(fx, fy):
        return my_x + (1 - 2 * my_x) * fx, my_y + (1 - 2 * my_y) * fy

    def copy_part(s, p, fx, fy):
        ix, iy = flipped(fx, fy)
        return pltpu.make_async_remote_copy(
            src_ref=part_send.at[s], dst_ref=part_got.at[s, my_id], send_sem=send_p.at[s, p],
            recv_sem=recv_p.at[s, p], device_id=(me_x + ix - my_x, me_y + iy - my_y),
            device_id_type=MESH,
        )

    def take_part(s, p, fx, fy):
        ix, iy = flipped(fx, fy)
        return pltpu.make_async_remote_copy(
            src_ref=part_send.at[s], dst_ref=part_got.at[s, ix * 2 + iy], send_sem=send_p.at[s, p],
            recv_sem=recv_p.at[s, p], device_id=(me_x + ix - my_x, me_y + iy - my_y),
            device_id_type=MESH,
        )

    def copy_group(i, g):
        x, y = group_xy(g)
        return pltpu.make_async_remote_copy(
            src_ref=fin.at[i], dst_ref=gathered.at[i, my_group], send_sem=send_g.at[i, g],
            recv_sem=recv_g.at[i, my_group], device_id=(x, y), device_id_type=MESH,
        )

    def take_group(i, g):
        x, y = group_xy(g)
        return pltpu.make_async_remote_copy(
            src_ref=fin.at[i], dst_ref=gathered.at[i, g], send_sem=send_g.at[i, g],
            recv_sem=recv_g.at[i, g], device_id=(x, y), device_id_type=MESH,
        )

    def share(i, rows):
        fin[i] = rows
        gathered[i, my_group] = rows

        @pl.loop(0, groups)
        def _(g):
            @pl.when(g != my_group)
            def _():
                copy_group(i, g).start()

    def length(m, own, x, h, y, store_x=None):
        dx, dy, dz = HALF[m]
        if dz == 2:
            near = [u_pp[c, x - 2, h, pl.ds(y - 8, 8), :] for c in range(3)]
        else:
            ref = u_p if dz else u_0
            near = [ref[c, x + dx, h, pl.ds(y + dy, 8), :] for c in range(3)]
        d = [near[c] - own[c] for c in range(3)]
        q = d[0] * d[0] + d[1] * d[1] + d[2] * d[2]
        rr[m, x, h, pl.ds(y, 8), :] = (
            q * lax.rsqrt(jnp.maximum(q, tiny)) - math.sqrt(square(HALF[m]))
        )

    def lengths(ms, x, h, y):
        own = [u_0[c, x, h, pl.ds(y, 8), :] for c in range(3)]
        for m in ms:
            length(m, own, x, h, y)

    every = list(range(PAIRS))
    dx_up = [m for m in every if HALF[m][0] == 1]
    dx_down = [m for m in every if HALF[m][0] == -1]
    x_two = INDEX[(2, 0, 0)]
    dy_up = [m for m in every if HALF[m][1] > 0]
    dy_down = [m for m in every if HALF[m][1] < 0]

    def inner_lengths():
        @pl.loop(0, nx)
        def _(x):
            for h in range(halves):
                for t in range(tiles):
                    lengths(every, x + 2, h, 8 + 8 * t)

    def side_lengths(base):
        for h in range(halves):
            for t in range(tiles):
                y = 8 + 8 * t
                lengths(dx_up, base + 1, h, y)
                lengths(dx_down, base + 2, h, y)

    def far_lengths(base):
        for h in range(halves):
            for t in range(tiles):
                lengths([x_two], base, h, 8 + 8 * t)
                lengths([x_two], base + 1, h, 8 + 8 * t)

    def edge_lengths():
        def one(ups, downs, x):
            for h in range(halves):
                for base in (0, ny):
                    if ups:
                        lengths(ups, x, h, base)
                    if downs:
                        lengths(downs, x, h, base + 8)

        @pl.loop(0, nx)
        def _(x):
            one(dy_up, dy_down, x + 2)

        one([m for m in dy_up if m in dx_up], [m for m in dy_down if m in dx_up], 1)
        one([m for m in dy_up if m in dx_down], [m for m in dy_down if m in dx_down], nx + 2)

    def plane_sums(c):
        sx = [c[i][0] + c[i][1] + c[i][2] for i in range(3)]
        fy = (c[0][2] + c[1][2] + c[2][2]) - (c[0][0] + c[1][0] + c[2][0])
        return [sx[2] - sx[0], fy, sx[0] + sx[1] + sx[2]]

    def forces(x, t):
        y = 8 + 8 * t
        rows = slice(8 * t, 8 * t + 8)
        total, back, back_two = [], [], []
        for h in range(halves):
            def forth(e):
                m = INDEX[e]
                return rr[m, x + 2, h, y : y + 8, :] * factors[m, x, h, rows, :]

            def behind(e):
                m = INDEX[e]
                at = y - e[1]
                return rr[m, x + 2 - e[0], h, at : at + 8, :] * factors[PAIRS + m, x, h, rows, :]

            up = plane_sums([[forth((dx, dy, 1)) for dy in (-1, 0, 1)] for dx in (-1, 0, 1)])
            down = plane_sums([[behind((dx, dy, 1)) for dy in (-1, 0, 1)] for dx in (-1, 0, 1)])

            def net(e):
                return forth(e) - behind(e)

            a, b = net((1, 1, 0)), net((1, -1, 0))
            fx = (a + b) + (net((1, 0, 0)) + net((2, 0, 0)))
            fy = (a - b) + (net((0, 1, 0)) + net((0, 2, 0)))
            total.append([up[0] + fx, up[1] + fy, up[2] + forth((0, 0, 2))])
            back.append(down)
            back_two.append(behind((0, 0, 2)))
        for c in range(3):
            for h, p in enumerate(shifted([back[h][c] for h in range(halves)], -1)):
                total[h][c] = total[h][c] - p
        for h, p in enumerate(shifted(back_two, -2)):
            total[h][2] = total[h][2] - p
        for c in range(3):
            total[top][c] = total[top][c] + pf[c, x, rows, :]
        return total

    for a in range(3):
        for load in loads[a]:
            load.wait()

    def sweep(visit, after_edges, after_sides, after_layer):
        @pl.loop(0, nx)
        def _(x):
            for t in (0, tiles - 1):
                visit(x, t)

        after_edges()

        @pl.loop(0, 2)
        def _(i):
            for t in range(1, tiles - 1):
                visit(i * (nx - 1), t)
            after_layer(i * (nx - 1))

        after_sides()

        @pl.loop(1, nx - 1)
        def _(x):
            for t in range(1, tiles - 1):
                visit(x, t)
            after_layer(x)

    def send_edges(s):
        for k, (dx, dy) in enumerate(CORNERS):
            x = 2 if dx < 0 else nx + 1
            y = 8 if dy < 0 else ny + 7
            for c in range(3):
                for h in range(halves):
                    edges_c[s, k, c, h] = u_0[c, x, h, y : y + 1, :]
        for k, d in enumerate((1, -1)):
            @pl.when(exists(0, d))
            def _():
                copy_edge(s, k, d).start()
        for k, (dx, dy) in enumerate(CORNERS):
            @pl.when(exists(dx, dy))
            def _():
                copy_corner(s, k, dx, dy).start()

    def send_sides(s, j):
        for k, d in enumerate((1, -1)):
            @pl.when(exists(d, 0))
            def _():
                copy_side(s, k, d, j).start()

    def nothing(*args):
        pass

    def first_step(x, t):
        rows = slice(8 * t, 8 * t + 8)
        advance(0, x, t, [
            [vel[c, x, rows, zs(h)] + 0.5 * dt * acc[c, x, rows, zs(h)] for c in range(3)]
            for h in range(halves)
        ])

    def greeted():
        count = groups - 1
        for dx, dy in SIDES + CORNERS:
            count = count + jnp.where(exists(dx, dy), 1, 0)
        pl.semaphore_wait(barrier, count)
        send_edges(0)

    sweep(first_step, greeted, lambda: send_sides(0, 0), nothing)
    send_sides(0, 1)

    def build_factors():
        above = [
            (word_bits(lambda e: e[i] == -1), word_bits(lambda e: e[i] == -2),
             word_bits(lambda e: e[i] == 1), word_bits(lambda e: e[i] == 2))
            for i in range(3)
        ]

        def allowed(at, size, i, w):
            one_down, two_down, one_up, two_up = (bits[w] for bits in above[i])
            keep = jnp.where(at < 1, 255 & ~one_down, 255)
            keep = keep & jnp.where(at < 2, 255 & ~two_down, 255)
            keep = keep & jnp.where(at > size - 2, 255 & ~one_up, 255)
            return keep & jnp.where(at > size - 3, 255 & ~two_up, 255)

        for h in range(halves):
            for t in range(tiles):
                for w in range(4):
                    at_y = me_y * ny + t * 8 + row8
                    at_z = lane + h * LANES
                    valid[h, t, w] = allowed(at_y, splits * ny, 1, w) & allowed(at_z, nz, 2, w)

        for load in loads[3]:
            load.wait()

        @pl.loop(0, nx)
        def _(x):
            ok_x = [allowed(me_x * nx + x, slabs * nx, 0, w) for w in range(4)]
            for t in range(tiles):
                rows = slice(8 * t, 8 * t + 8)
                words = [
                    [mask_ref[w, x, rows, zs(h)] & (valid[h, t, w] & ok_x[w]) for w in range(4)]
                    for h in range(halves)
                ]
                moved = {0: words}
                for by in (1, 2):
                    cols = [shifted([words[h][w] for h in range(halves)], by) for w in range(4)]
                    moved[by] = [[cols[w][h] for w in range(4)] for h in range(halves)]
                for h in range(halves):
                    for m, e in enumerate(HALF):
                        scale = bond_stiffness / square(e) * (2.0 if square(e) == 4 else 1.0)
                        minus = (-e[0], -e[1], -e[2])
                        for at, bond, frame in ((m, e, 0), (PAIRS + m, minus, e[2])):
                            n = NUMBER[bond]
                            bit = moved[frame][h][n // 8] & (1 << (n % 8))
                            factors[at, x, h, rows, :] = jnp.where(bit != 0, scale, 0.0)

    wide_lane = lax.broadcasted_iota(jnp.int32, (LANES, LANES), 1).astype(f32)
    wide_row = lax.broadcasted_iota(jnp.int32, (LANES, LANES), 0).astype(f32)
    r16 = lax.broadcasted_iota(jnp.int32, (ROWS, LANES), 0)

    def padded(a):
        n = a.shape[0]
        return a if n == LANES else jnp.concatenate([a, jnp.zeros((LANES - n, LANES), f32)], axis=0)

    def column(row):
        return jnp.broadcast_to(row, (LANES, LANES)).T

    def build_tables():
        for load in small:
            load.wait()
        where = []
        for c, (size, most) in enumerate(((2 * nx, slabs // 2), (2 * ny, half_split))):
            sums = jnp.sum(padded(qpos_ref[c]).T, axis=0, keepdims=True)
            cell = jnp.floor((sums * (1.0 / PTS) + 0.5) * (1.0 / size))
            where.append(jnp.clip(cell, 0.0, float(most - 1)))
        group = where[0] * float(half_split) + where[1]
        same = (column(group) == group) & (wide_row < wide_lane)
        rank = jnp.sum(jnp.where(same, 1.0, 0.0), axis=0, keepdims=True)
        place = group * float(ROWS) + jnp.minimum(rank, float(per_group - 1))
        place = jnp.where(wide_lane[0:1] < float(blocks), place, -1e6)
        place_col[...] = column(place)
        first = (my_group * ROWS).astype(f32)
        wide_place = jnp.broadcast_to(place, (ROWS, LANES))
        of_slot = jnp.where(wide_place == first + (r16 // per_block).astype(f32), 1.0, 0.0)
        of_state = jnp.where(
            wide_place == first + lax.rem(r16, per_group).astype(f32), 1.0, 0.0
        )

        def mine(ref):
            out = jnp.zeros((ROWS, LANES), f32)
            for c in range(3):
                out = jnp.where(r16 // per_group == c, exact_dot(of_state, padded(ref[c])), out)
            return out

        half = mine(qvel_ref) + 0.5 * dt * mine(qacc_ref)
        qv[...] = half
        qp[...] = mine(qpos_ref) + dt * half

        pairs_s[...] = jnp.full(pairs_s.shape, -1, jnp.int32)
        for s in range(subs):
            pairs_s[2 * s : 2 * s + 2, 0:slots] = pairs_ref[s]
        earlier = jnp.where(wide_row < wide_lane, 1.0, 0.0)
        for s in range(subs):
            target = pairs_s[2 * s : 2 * s + 1].astype(f32)
            chosen = pairs_s[2 * s + 1 : 2 * s + 2].astype(f32)
            hit = exact_dot(of_slot, jnp.where(wide_row == chosen, 1.0, 0.0))
            order = exact_dot(hit, earlier)
            hit = jnp.where(order == lax.rem(r16, per_block).astype(f32), hit, 0.0)
            table = exact_dot(hit, jnp.where(column(target) * float(SL) == wide_lane, 1.0, 0.0))
            onehot[s] = table
            onehot_t[s] = padded(table).T
            live = jnp.sum(table, axis=1, keepdims=True)
            penalty[s] = jnp.broadcast_to(far * (1.0 - live), (ROWS, LANES))

    stretch = math.sqrt(1.0 / (math.log(2.0) * contact_width))
    strength = contact_stiffness / stretch

    def contact(s):
        base = jnp.where(
            r16 // per_group == 0, (me_x * nx + mid_x).astype(f32),
            jnp.where(r16 // per_group == 1, (me_y * ny + mid_y).astype(f32), float(nz - SL)),
        )
        rel = (qp[...] - base) * stretch
        for i in range(3 * per_group):
            qb[i] = column(rel[i : i + 1])
        for c in range(3):
            cols = []
            for t in range(tiles):
                col = zero_tile
                for x in range(nx):
                    tile = u_0[c, x + 2, top, 8 + 8 * t : 16 + 8 * t, :]
                    tile = pltpu.roll(tile, SL * x + SL, axis=1)
                    col = jnp.where(lane // SL == x, tile, col)
                cols.append(col)
            stack = []
            for z in range(SL):
                for col in cols:
                    col = pltpu.roll(col, (LANES - z) % LANES, axis=1) if z else col
                    stack.append(col + float(z) if c == 2 else col)
            table = exact_dot(onehot[s], jnp.concatenate(stack, axis=0).T * stretch)
            psel[c] = table + penalty[s] if c == 0 else table

        @pl.loop(0, per_group)
        def _(r):
            first = r * per_block
            points = [
                [jnp.broadcast_to(psel[c, pl.ds(first + j, 1), :], (8, LANES)) for c in range(3)]
                for j in range(per_block)
            ]
            on_points = [[zero_tile] * 3 for _ in range(per_block)]
            for i in range(PTS // 8):
                rows = slice(8 * i, 8 * i + 8)
                q = [qb[c * per_group + r, rows, :] for c in range(3)]
                pulls = [None] * 3
                for j in range(per_block):
                    d = [points[j][c] - q[c] for c in range(3)]
                    w = jnp.exp2(-(d[0] * d[0] + d[1] * d[1] + d[2] * d[2]))
                    for c in range(3):
                        pull = w * d[c]
                        pulls[c] = pull if pulls[c] is None else pulls[c] + pull
                        on_points[j][c] = on_points[j][c] + pull
                for c in range(3):
                    qb[c * per_group + r, rows, :] = pulls[c]
            for j in range(per_block):
                for c in range(3):
                    slot_rows[c, pl.ds(first + j, 1), :] = strength * jnp.sum(
                        on_points[j][c], axis=0, keepdims=True
                    )

        for i in range(3 * per_group):
            row = -strength * jnp.sum(qb[i].T, axis=0, keepdims=True)
            part_send[s, i : i + 1] = row
            part_got[s, my_id, i : i + 1] = row
        for p, (fx, fy) in enumerate(partners):
            copy_part(s, p, fx, fy).start()

        for c in range(3):
            spread = exact_dot(onehot_t[s], slot_rows[c]).T
            for t in range(tiles):
                packed = zero_tile
                for z in range(SL):
                    tile = spread[z * ny + 8 * t : z * ny + 8 * t + 8]
                    tile = pltpu.roll(tile, z, axis=1) if z else tile
                    packed = jnp.where(lax.rem(lane, SL) == z, tile, packed)
                for x in range(nx):
                    tile = pltpu.roll(packed, LANES - SL - SL * x, axis=1) if x < nx else packed
                    pf[c, x, 8 * t : 8 * t + 8, :] = jnp.where(lane >= LANES - SL, tile, 0.0)

    def particle_force(s):
        for p, (fx, fy) in enumerate(partners):
            take_part(s, p, fx, fy).wait()
        total = part_got[s, 0] + part_got[s, 1] + part_got[s, 2] + part_got[s, 3]
        return inverse_mass * total

    slot_rows[...] = jnp.zeros(slot_rows.shape, f32)
    part_send[...] = jnp.zeros(part_send.shape, f32)
    for s in range(subs):
        part_got[s, my_id] = jnp.zeros(part_got.shape[2:], f32)

    def put_side(s, k, j):
        d = (-1, 1)[k]
        x = 1 - j if d < 0 else nx + 2 + j
        for c in range(3):
            parts = [got_x[s, k, j, c, h] for h in range(halves)]
            if c == 0:
                parts = [p + float(d * nx) for p in parts]
            put(c, x, slice(8, 8 + ny), parts, j == 0)

    def put_corner(s, dx, dy):
        j = CORNERS.index((-dx, -dy))
        take_corner(s, j, dx, dy).wait_recv()
        x = 1 if dx < 0 else nx + 2
        y = 7 if dy < 0 else ny + 8
        for c in range(3):
            parts = [got_c[s, j, c, h] for h in range(halves)]
            if c == 0:
                parts = [p + float(dx * nx) for p in parts]
            if c == 1:
                parts = [p + float(dy * ny) for p in parts]
            put(c, x, slice(y, y + 1), parts)

    def put_edge(s, k, d):
        take_edge(s, k, d).wait_recv()

        @pl.loop(0, nx)
        def _(x):
            for c in range(3):
                parts = [got_y[s, k, c, x, h] for h in range(halves)]
                if c == 1:
                    parts = [p + float(d * ny) for p in parts]
                y = 6 if d < 0 else ny + 8
                put(c, x + 2, slice(y, y + 2), parts)

    def sent(s):
        for k, d in enumerate((1, -1)):
            @pl.when(exists(d, 0))
            def _():
                for j in range(2):
                    copy_side(s, k, d, j).wait_send()

            @pl.when(exists(0, d))
            def _():
                copy_edge(s, k, d).wait_send()
        for k, (dx, dy) in enumerate(CORNERS):
            @pl.when(exists(dx, dy))
            def _():
                copy_corner(s, k, dx, dy).wait_send()

    def substep(s):
        last = s == subs - 1

        @pl.when(s == 0)
        def _():
            build_tables()

        @pl.when(s > 0)
        def _():
            half = qv[...] + dt * particle_force(s - 1)
            qv[...] = half
            qp[...] = qp[...] + dt * half

        @pl.when(last)
        def _():
            share(0, qp[...])
            for c in range(3):
                pltpu.make_async_copy(dsp.at[c], disp_out.at[c], out_sem.at[0, c]).start()

        contact(s)
        inner_lengths()

        @pl.when(s == 0)
        def _():
            build_factors()

        for k, d in enumerate((-1, 1)):
            @pl.when(exists(d, 0))
            def _():
                take_side(s, k, 0).wait_recv()
                put_side(s, k, 0)
        for dx, dy in CORNERS:
            @pl.when(exists(dx, dy))
            def _():
                put_corner(s, dx, dy)
        for k, d in enumerate((-1, 1)):
            @pl.when(exists(0, d))
            def _():
                put_edge(s, k, d)

        @pl.loop(0, 2)
        def _(i):
            side_lengths(i * nx)

        edge_lengths()

        for k, d in enumerate((-1, 1)):
            @pl.when(exists(d, 0))
            def _():
                take_side(s, k, 1).wait_recv()
                put_side(s, k, 1)

        @pl.loop(0, 2)
        def _(i):
            far_lengths(i * nx)

        sent(s)

        @pl.when(s < subs - 1)
        def _():
            def visit(x, t):
                rows = slice(8 * t, 8 * t + 8)
                total = forces(x, t)
                advance(s + 1, x, t, [
                    [vel[c, x, rows, zs(h)] + dt * total[h][c] for c in range(3)]
                    for h in range(halves)
                ])

            sweep(visit, lambda: send_edges(s + 1), lambda: send_sides(s + 1, 0), nothing)
            send_sides(s + 1, 1)

        @pl.when(last)
        def _():
            share(1, qv[...] + 0.5 * dt * particle_force(s))

            def visit(x, t):
                rows = slice(8 * t, 8 * t + 8)
                total = forces(x, t)
                for h in range(halves):
                    for c in range(3):
                        vel[c, x, rows, zs(h)] = vel[c, x, rows, zs(h)] + 0.5 * dt * total[h][c]

            def leave(x):
                pltpu.make_async_copy(vel.at[:, x], vel_out.at[:, x], out_sem.at[1, x]).start()

            sweep(visit, nothing, nothing, leave)

    @pl.loop(0, subs)
    def _(s):
        substep(s)

    where = place_col[0:blocks]
    for i, dst in enumerate((pos_out, pvel_out)):
        @pl.loop(0, groups)
        def _(g):
            @pl.when(g != my_group)
            def _():
                take_group(i, g).wait()

        for c in range(3):
            out = None
            for k in range(0, groups * ROWS, LANES):
                rows = gathered[i, k // ROWS : (k + LANES) // ROWS].reshape(-1, LANES)
                pick = jnp.where(
                    where + float(c * per_group - k) == wide_lane[0:blocks], 1.0, 0.0
                )[:, 0 : rows.shape[0]]
                part = exact_dot(pick, rows)
                out = part if out is None else out + part
            ends[i, c] = out
        pltpu.make_async_copy(ends.at[i], dst, end_sem.at[i]).start()

    for c in range(3):
        pltpu.make_async_copy(dsp.at[c], disp_out.at[c], out_sem.at[0, c]).wait()

    @pl.loop(0, nx)
    def _(x):
        pltpu.make_async_copy(vel.at[:, x], vel_out.at[:, x], out_sem.at[1, x]).wait()

    for i, dst in enumerate((pos_out, pvel_out)):
        pltpu.make_async_copy(ends.at[i], dst, end_sem.at[i]).wait()


def finish_kernel(n, *refs):
    held, sem = refs[2 * n : 3 * n], refs[-1]
    loads = [pltpu.make_async_copy(refs[i], held[i], sem.at[0, i]) for i in range(n)]
    stores = [pltpu.make_async_copy(held[i], refs[n + i], sem.at[1, i]) for i in range(n)]
    for load in loads:
        load.start()
    for load, store in zip(loads, stores):
        load.wait()
        store.start()
    for store in stores:
        store.wait()


def finish(*arrays):
    anywhere = pl.BlockSpec(memory_space=pl.ANY)
    n = len(arrays)
    return pl.pallas_call(
        functools.partial(finish_kernel, n),
        out_shape=tuple(jax.ShapeDtypeStruct(a.shape, a.dtype) for a in arrays),
        in_specs=[anywhere] * n,
        out_specs=(anywhere,) * n,
        scratch_shapes=[pltpu.VMEM(a.shape, a.dtype) for a in arrays]
        + [pltpu.SemaphoreType.DMA((2, n))],
        compiler_params=pltpu.CompilerParams(vmem_limit_bytes=60 * 1024 * 1024),
    )(*arrays)


def per_device(
    slabs, splits,
    displacement, velocity, acceleration, bond_masks, proj_pos, proj_vel, proj_acc, contact_pairs
):
    _, nx, ny, nz = displacement.shape
    subs = contact_pairs.shape[0]
    blocks = proj_pos.shape[0]
    groups = (slabs // 2) * (splits // 2)
    per_group = blocks // groups
    halves = nz // LANES
    assert nx == SB_DEV and ny * SL == PTS and ny % 8 == 0
    assert per_group * 3 <= ROWS and blocks <= LANES and contact_pairs.shape[2] <= ROWS
    assert (groups * ROWS) % LANES == 0 or groups * ROWS < LANES

    dims = (subs, nx, ny, nz, slabs, splits, per_group, blocks)
    anywhere = pl.BlockSpec(memory_space=pl.ANY)
    padded = (3, nx + 4, halves, ny + 16, LANES)
    block = (3, nx, ny, nz)
    dma = pltpu.SemaphoreType.DMA
    scratch = [
        pltpu.VMEM((3, blocks, PTS), f32),
        pltpu.VMEM((3, blocks, PTS), f32),
        pltpu.VMEM((3, blocks, PTS), f32),
        pltpu.VMEM(contact_pairs.shape, jnp.int32),
        pltpu.VMEM((2, 3, blocks, PTS), f32),
        pltpu.VMEM(padded, f32),
        pltpu.VMEM(padded, f32),
        pltpu.VMEM((3, nx, halves, ny, LANES), f32),
        pltpu.VMEM(block, f32),
        pltpu.VMEM(block, f32),
        pltpu.VMEM(block, f32),
        pltpu.VMEM((4, nx, ny, nz), jnp.int32),
        pltpu.VMEM((halves, ny // 8, 4, 8, LANES), jnp.int32),
        pltpu.VMEM((2 * PAIRS, nx, halves, ny, LANES), f32),
        pltpu.VMEM((PAIRS, nx + 3, halves, ny + 16, LANES), f32),
        pltpu.VMEM((subs, 2, 3, nx, halves, 2, LANES), f32),
        pltpu.VMEM((subs, 4, 3, halves, 1, LANES), f32),
        pltpu.VMEM((subs, 2, 2, 3, halves, ny, LANES), f32),
        pltpu.VMEM((subs, 2, 3, nx, halves, 2, LANES), f32),
        pltpu.VMEM((subs, 4, 3, halves, 1, LANES), f32),
        pltpu.VMEM((3 * per_group, PTS, LANES), f32),
        pltpu.VMEM((3, ROWS, LANES), f32),
        pltpu.VMEM((3, LANES, LANES), f32),
        pltpu.VMEM((3, nx, ny, LANES), f32),
        pltpu.VMEM((8, LANES), jnp.int32),
        pltpu.VMEM((subs, ROWS, LANES), f32),
        pltpu.VMEM((subs, LANES, LANES), f32),
        pltpu.VMEM((subs, ROWS, LANES), f32),
        pltpu.VMEM((LANES, LANES), f32),
        pltpu.VMEM((ROWS, LANES), f32),
        pltpu.VMEM((ROWS, LANES), f32),
        pltpu.VMEM((subs, ROWS, LANES), f32),
        pltpu.VMEM((subs, 4, ROWS, LANES), f32),
        pltpu.VMEM((2, ROWS, LANES), f32),
        pltpu.VMEM((2, groups, ROWS, LANES), f32),
        dma((4, 2)), dma((4,)), dma((2, nx)), dma((2,)),
        dma((subs, 2, 2)), dma((subs, 2, 2)), dma((subs, 2)), dma((subs, 2)),
        dma((subs, 4)), dma((subs, 4)), dma((subs, 3)), dma((subs, 3)),
        dma((2, groups)), dma((2, groups)),
    ]
    moved, speed, points, point_speed = pl.pallas_call(
        functools.partial(kernel, dims),
        out_shape=(
            jax.ShapeDtypeStruct(displacement.shape, f32),
            jax.ShapeDtypeStruct(displacement.shape, f32),
            jax.ShapeDtypeStruct((3, blocks, PTS), f32),
            jax.ShapeDtypeStruct((3, blocks, PTS), f32),
        ),
        in_specs=[anywhere] * 8,
        out_specs=(anywhere,) * 4,
        scratch_shapes=scratch,
        compiler_params=pltpu.CompilerParams(
            collective_id=0, has_side_effects=True, vmem_limit_bytes=60 * 1024 * 1024
        ),
    )(
        displacement, velocity, acceleration, bond_masks,
        jnp.moveaxis(proj_pos, 1, 0), jnp.moveaxis(proj_vel, 1, 0), jnp.moveaxis(proj_acc, 1, 0),
        contact_pairs,
    )
    moved, speed, points, point_speed = finish(moved, speed, points, point_speed)
    return moved, speed, jnp.moveaxis(points, 0, 1), jnp.moveaxis(point_speed, 0, 1)


def solution(mesh):
    cells = P(None, "slab", "split", None)
    return jax.shard_map(
        functools.partial(per_device, mesh.shape["slab"], mesh.shape["split"]),
        mesh=mesh,
        in_specs=(cells, cells, cells, cells, P(), P(), P(), P(None, None, ("slab", "split"))),
        out_specs=(cells, cells, P(), P()),
        check_vma=False,
    )
```

```python
import functools
import math

import jax
import jax.numpy as jnp
from jax import lax
from jax.experimental import pallas as pl
from jax.experimental.pallas import tpu as pltpu
from jax.sharding import PartitionSpec as P

SL = 4
PTS = 128
SB_DEV = 8
LANES = 128
ROWS = 16

time_step = 0.25
bond_stiffness = 0.5
contact_stiffness = 0.05
contact_width = 8.0
inverse_mass = 0.5
tiny = 1e-30
far = 1e4
MESH = pl.DeviceIdType.MESH
f32 = jnp.float32
bf16 = jnp.bfloat16


def bond_offsets():
    listed = []
    for shift_x in (-2, -1, 0, 1, 2):
        for shift_y in (-2, -1, 0, 1, 2):
            for shift_z in (-2, -1, 0, 1, 2):
                squared = shift_x * shift_x + shift_y * shift_y + shift_z * shift_z
                if 0 < squared <= 4:
                    listed.append((shift_x, shift_y, shift_z))
    return listed


OFFSETS = bond_offsets()
NUMBER = {e: n for n, e in enumerate(OFFSETS)}
HALF = [(dx, dy, 1) for dx in (-1, 0, 1) for dy in (-1, 0, 1)] + [(0, 0, 2)] + [
    (1, 0, 0), (2, 0, 0), (0, 1, 0), (0, 2, 0), (1, 1, 0), (1, -1, 0)
]
INDEX = {e: m for m, e in enumerate(HALF)}
PAIRS = len(HALF)
CORNERS = [(-1, -1), (-1, 1), (1, -1), (1, 1)]
SIDES = [(-1, 0), (1, 0), (0, -1), (0, 1)]


def square(e):
    return e[0] * e[0] + e[1] * e[1] + e[2] * e[2]


def word_bits(test):
    words = [0, 0, 0, 0]
    for n, e in enumerate(OFFSETS):
        if test(e):
            words[n // 8] |= 1 << (n % 8)
    return words


def plain_dot(a, b):
    return lax.dot_general(a, b, (((1,), (0,)), ((), ())), preferred_element_type=f32)


def exact_dot(a, b):
    return lax.dot_general(
        a, b, (((1,), (0,)), ((), ())), precision=lax.Precision.HIGHEST, preferred_element_type=f32
    )


def kernel(
    dims,
    disp_hbm, vel_hbm, acc_hbm, mask_hbm, qpos_hbm, qvel_hbm, qacc_hbm, pairs_hbm,
    disp_out, vel_out, pos_out, pvel_out,
    qpos_ref, qvel_ref, qacc_ref, pairs_ref, ends,
    u_0, u_p, u_pp, dsp, vel, acc, mask_ref, valid, factors, rr, edges_y, edges_c,
    got_x, got_y, got_c, qb, spread_row, sum_column, psel, slot_rows, pf, pairs_s, onehot, onehot_t, penalty, place_col,
    qp, qv, part_send, part_got, fin, gathered,
    in_sem, small_sem, out_sem, end_sem, send_x, recv_x, send_y, recv_y, send_c, recv_c, send_p, recv_p, send_g, recv_g,
):
    subs, nx, ny, nz, slabs, splits, per_group, blocks = dims
    halves = nz // LANES
    tiles = ny // 8
    slots = pairs_ref.shape[2]
    per_block = slots // per_group
    top = halves - 1
    me_x = lax.axis_index("slab")
    me_y = lax.axis_index("split")
    mid_x, mid_y = nx // 2, ny // 2
    half_split = splits // 2
    groups = (slabs // 2) * half_split
    my_group = (me_x // 2) * half_split + me_y // 2
    my_x, my_y = lax.rem(me_x, 2), lax.rem(me_y, 2)
    my_id = my_x * 2 + my_y
    dt = time_step

    def exists(dx, dy):
        ok = None
        for d, me, n in ((dx, me_x, slabs), (dy, me_y, splits)):
            if d:
                cond = (me > 0) if d < 0 else (me < n - 1)
                ok = cond if ok is None else ok & cond
        return ok

    cut = nx // 2
    loads = [
        [
            pltpu.make_async_copy(
                src.at[:, i * cut : (i + 1) * cut], dst.at[:, i * cut : (i + 1) * cut, 0:ny],
                in_sem.at[a, i],
            )
            for i in range(2)
        ]
        for a, (src, dst) in enumerate(
            ((acc_hbm, acc), (vel_hbm, vel), (disp_hbm, dsp), (mask_hbm, mask_ref))
        )
    ]

    small = [
        pltpu.make_async_copy(src, dst, small_sem.at[i])
        for i, (src, dst) in enumerate((
            (qpos_hbm, qpos_ref), (qvel_hbm, qvel_ref), (qacc_hbm, qacc_ref), (pairs_hbm, pairs_ref)
        ))
    ]
    for load in small:
        load.start()
    for a in range(4):
        for load in loads[a]:
            load.start()

    barrier = pltpu.get_barrier_semaphore()

    def greet(x, y):
        pl.semaphore_signal(barrier, inc=1, device_id=(x, y), device_id_type=MESH)

    for dx, dy in SIDES + CORNERS:
        @pl.when(exists(dx, dy))
        def _():
            greet(me_x + dx, me_y + dy)

    def group_xy(g):
        return 2 * (g // half_split) + my_x, 2 * lax.rem(g, half_split) + my_y

    @pl.loop(0, groups)
    def _(g):
        @pl.when(g != my_group)
        def _():
            x, y = group_xy(g)
            greet(x, y)

    lane = lax.broadcasted_iota(jnp.int32, (8, LANES), 1)
    row8 = lax.broadcasted_iota(jnp.int32, (8, LANES), 0)
    zero_tile = jnp.zeros((8, LANES), f32)

    for ref in (u_0, u_p):
        for x in (0, 1, nx + 2, nx + 3):
            ref[:, x] = jnp.zeros(ref.shape[:1] + ref.shape[2:], f32)

        @pl.loop(2, nx + 2)
        def _(x):
            for c in range(3):
                for h in range(halves):
                    ref[c, x, h, 0:8, :] = zero_tile
                    ref[c, x, h, ny + 8 : ny + 16, :] = zero_tile

    def shifted(parts, by):
        rows = parts[0].shape[0]
        lanes = lax.broadcasted_iota(jnp.int32, (rows, LANES), 1)
        rolled = [pltpu.roll(p, (-by) % LANES, axis=1) for p in parts]
        out = []
        n = len(parts)
        for h in range(n):
            other = (h + 1) % n if by > 0 else (h - 1) % n
            edge = lanes >= LANES - by if by > 0 else lanes < -by
            out.append(jnp.where(edge, rolled[other], rolled[h]))
        return out

    def put(c, x, rows, parts, shifts=True):
        for h, p in enumerate(parts):
            u_0[c, x, h, rows, :] = p
        if shifts:
            for h, p in enumerate(shifted(parts, 1)):
                u_p[c, x, h, rows, :] = p + 1.0 if c == 2 else p

    def zs(h):
        return slice(h * LANES, (h + 1) * LANES)

    def advance(s, x, t, speeds):
        rows = slice(8 * t, 8 * t + 8)
        for c in range(3):
            parts = []
            for h in range(halves):
                half = speeds[h][c]
                vel[c, x, rows, zs(h)] = half
                moved = dsp[c, x, rows, zs(h)] + dt * half
                dsp[c, x, rows, zs(h)] = moved
                if c == 0:
                    moved = moved + (x - mid_x).astype(f32)
                elif c == 1:
                    moved = moved + (row8 + (8 * t - mid_y)).astype(f32)
                parts.append(moved)
            put(c, x + 2, slice(8 + 8 * t, 16 + 8 * t), parts)
            for h, p in enumerate(shifted(parts, 2)):
                u_pp[c, x, h, rows, :] = p + 2.0 if c == 2 else p
            for h, p in enumerate(parts):
                for j in range(2):
                    if t == 0:
                        edges_y[s, 0, j, c, h, pl.ds(x, 1), :] = p[j : j + 1]
                    if t == tiles - 1:
                        edges_y[s, 1, j, c, h, pl.ds(x, 1), :] = p[7 - j : 8 - j]

    def near_layer(d):
        return 0 if d < 0 else nx - 1

    def copy_side(s, k, d, j):
        layer = near_layer(d) - d * j
        return pltpu.make_async_remote_copy(
            src_ref=u_0.at[:, 2 + layer, :, 8 : 8 + ny, :], dst_ref=got_x.at[s, k, j],
            send_sem=send_x.at[s, k, j], recv_sem=recv_x.at[s, k, j],
            device_id=(me_x + d, me_y), device_id_type=MESH,
        )

    def take_side(s, k, j):
        d = (-1, 1)[k]
        return pltpu.make_async_remote_copy(
            src_ref=got_x.at[s, k, j], dst_ref=got_x.at[s, k, j],
            send_sem=send_x.at[s, k, j], recv_sem=recv_x.at[s, k, j],
            device_id=(me_x + d, me_y), device_id_type=MESH,
        )

    def copy_edge(s, k, d, j):
        return pltpu.make_async_remote_copy(
            src_ref=edges_y.at[s, 1 - k, j], dst_ref=got_y.at[s, k, j],
            send_sem=send_y.at[s, k, j], recv_sem=recv_y.at[s, k, j],
            device_id=(me_x, me_y + d), device_id_type=MESH,
        )

    def take_edge(s, k, d, j):
        return pltpu.make_async_remote_copy(
            src_ref=got_y.at[s, k, j], dst_ref=got_y.at[s, k, j], send_sem=send_y.at[s, k, j],
            recv_sem=recv_y.at[s, k, j], device_id=(me_x, me_y + d), device_id_type=MESH,
        )

    def copy_corner(s, k, dx, dy):
        return pltpu.make_async_remote_copy(
            src_ref=edges_c.at[s, k], dst_ref=got_c.at[s, k], send_sem=send_c.at[s, k],
            recv_sem=recv_c.at[s, k], device_id=(me_x + dx, me_y + dy), device_id_type=MESH,
        )

    def take_corner(s, j, dx, dy):
        return pltpu.make_async_remote_copy(
            src_ref=got_c.at[s, j], dst_ref=got_c.at[s, j], send_sem=send_c.at[s, j],
            recv_sem=recv_c.at[s, j], device_id=(me_x + dx, me_y + dy), device_id_type=MESH,
        )

    partners = ((0, 1), (1, 0), (1, 1))

    def flipped(fx, fy):
        return my_x + (1 - 2 * my_x) * fx, my_y + (1 - 2 * my_y) * fy

    def copy_part(s, p, fx, fy):
        ix, iy = flipped(fx, fy)
        return pltpu.make_async_remote_copy(
            src_ref=part_send.at[s], dst_ref=part_got.at[s, my_id], send_sem=send_p.at[s, p],
            recv_sem=recv_p.at[s, p], device_id=(me_x + ix - my_x, me_y + iy - my_y),
            device_id_type=MESH,
        )

    def take_part(s, p, fx, fy):
        ix, iy = flipped(fx, fy)
        return pltpu.make_async_remote_copy(
            src_ref=part_send.at[s], dst_ref=part_got.at[s, ix * 2 + iy], send_sem=send_p.at[s, p],
            recv_sem=recv_p.at[s, p], device_id=(me_x + ix - my_x, me_y + iy - my_y),
            device_id_type=MESH,
        )

    def copy_group(i, g):
        x, y = group_xy(g)
        return pltpu.make_async_remote_copy(
            src_ref=fin.at[i], dst_ref=gathered.at[i, my_group], send_sem=send_g.at[i, g],
            recv_sem=recv_g.at[i, my_group], device_id=(x, y), device_id_type=MESH,
        )

    def take_group(i, g):
        x, y = group_xy(g)
        return pltpu.make_async_remote_copy(
            src_ref=fin.at[i], dst_ref=gathered.at[i, g], send_sem=send_g.at[i, g],
            recv_sem=recv_g.at[i, g], device_id=(x, y), device_id_type=MESH,
        )

    def share(i, rows):
        fin[i] = rows
        gathered[i, my_group] = rows

        @pl.loop(0, groups)
        def _(g):
            @pl.when(g != my_group)
            def _():
                copy_group(i, g).start()

    def length(m, own, x, h, y):
        dx, dy, dz = HALF[m]
        if dz == 2:
            near = [u_pp[c, x - 2, h, pl.ds(y - 8, 8), :] for c in range(3)]
        else:
            ref = u_p if dz else u_0
            near = [ref[c, x + dx, h, pl.ds(y + dy, 8), :] for c in range(3)]
        d = [near[c] - own[c] for c in range(3)]
        q = d[0] * d[0] + d[1] * d[1] + d[2] * d[2]
        rr[m, x, pl.ds(h * (ny + 16) + y, 8), :] = (
            q * lax.rsqrt(jnp.maximum(q, tiny)) - math.sqrt(square(HALF[m]))
        )

    def lengths(ms, x, h, y):
        own = [u_0[c, x, h, pl.ds(y, 8), :] for c in range(3)]
        for m in ms:
            length(m, own, x, h, y)

    every = list(range(PAIRS))
    dx_up = [m for m in every if HALF[m][0] == 1]
    dx_down = [m for m in every if HALF[m][0] == -1]
    x_two = INDEX[(2, 0, 0)]
    y_two = INDEX[(0, 2, 0)]
    dy_up = [m for m in every if HALF[m][1] == 1]
    dy_down = [m for m in every if HALF[m][1] < 0]

    def inner_lengths():
        @pl.loop(0, nx, unroll=2)
        def _(x):
            for h in range(halves):
                for t in range(tiles):
                    lengths(every, x + 2, h, 8 + 8 * t)

    def side_lengths(base):
        for h in range(halves):
            for t in range(tiles):
                y = 8 + 8 * t
                lengths(dx_up, base + 1, h, y)
                lengths(dx_down, base + 2, h, y)

    def far_lengths(base):
        for h in range(halves):
            for t in range(tiles):
                lengths([x_two], base, h, 8 + 8 * t)
                lengths([x_two], base + 1, h, 8 + 8 * t)

    def edge_lengths():
        def one(ups, downs, x):
            for h in range(halves):
                for base in (0, ny):
                    if ups:
                        lengths(ups, x, h, base)
                    if downs:
                        lengths(downs, x, h, base + 8)

        @pl.loop(0, nx, unroll=2)
        def _(x):
            one(dy_up, dy_down, x + 2)

        one([m for m in dy_up if m in dx_up], [m for m in dy_down if m in dx_up], 1)
        one([m for m in dy_up if m in dx_down], [m for m in dy_down if m in dx_down], nx + 2)

    def plane_sums(c):
        sx = [c[i][0] + c[i][1] + c[i][2] for i in range(3)]
        fy = (c[0][2] + c[1][2] + c[2][2]) - (c[0][0] + c[1][0] + c[2][0])
        return [sx[2] - sx[0], fy, sx[0] + sx[1] + sx[2]]

    def forces(x, t):
        y = 8 + 8 * t
        rows = slice(8 * t, 8 * t + 8)
        total, back, back_two = [], [], []
        for h in range(halves):
            def forth(e):
                m = INDEX[e]
                at = h * (ny + 16) + y
                return rr[m, x + 2, at : at + 8, :] * factors[x, h, t, m]

            def behind(e):
                m = INDEX[e]
                at = h * (ny + 16) + y - e[1]
                return rr[m, x + 2 - e[0], at : at + 8, :] * factors[x, h, t, PAIRS + m]

            up = plane_sums([[forth((dx, dy, 1)) for dy in (-1, 0, 1)] for dx in (-1, 0, 1)])
            down = plane_sums([[behind((dx, dy, 1)) for dy in (-1, 0, 1)] for dx in (-1, 0, 1)])

            def net(e):
                return forth(e) - behind(e)

            a, b = net((1, 1, 0)), net((1, -1, 0))
            fx = (a + b) + (net((1, 0, 0)) + net((2, 0, 0)))
            fy = (a - b) + (net((0, 1, 0)) + net((0, 2, 0)))
            total.append([up[0] + fx, up[1] + fy, up[2] + forth((0, 0, 2))])
            back.append(down)
            back_two.append(behind((0, 0, 2)))
        for c in range(3):
            for h, p in enumerate(shifted([back[h][c] for h in range(halves)], -1)):
                total[h][c] = total[h][c] - p
        for h, p in enumerate(shifted(back_two, -2)):
            total[h][2] = total[h][2] - p
        for c in range(3):
            total[top][c] = total[top][c] + pf[c, x, rows, :]
        return total

    wide_lane = lax.broadcasted_iota(jnp.int32, (LANES, LANES), 1).astype(f32)
    wide_row = lax.broadcasted_iota(jnp.int32, (LANES, LANES), 0).astype(f32)
    r16 = lax.broadcasted_iota(jnp.int32, (ROWS, LANES), 0)

    def padded(a):
        n = a.shape[0]
        return a if n == LANES else jnp.concatenate([a, jnp.zeros((LANES - n, LANES), f32)], axis=0)

    def column(row):
        return jnp.broadcast_to(row, (LANES, LANES)).T

    def build_tables():
        for load in small:
            load.wait()
        where = []
        for c, (size, most) in enumerate(((2 * nx, slabs // 2), (2 * ny, half_split))):
            sums = jnp.sum(padded(qpos_ref[c]).T, axis=0, keepdims=True)
            cell = jnp.floor((sums * (1.0 / PTS) + 0.5) * (1.0 / size))
            where.append(jnp.clip(cell, 0.0, float(most - 1)))
        group = where[0] * float(half_split) + where[1]
        same = (column(group) == group) & (wide_row < wide_lane)
        rank = jnp.sum(jnp.where(same, 1.0, 0.0), axis=0, keepdims=True)
        place = group * float(ROWS) + jnp.minimum(rank, float(per_group - 1))
        place = jnp.where(wide_lane[0:1] < float(blocks), place, -1e6)
        place_col[...] = column(place)
        first = (my_group * ROWS).astype(f32)
        wide_place = jnp.broadcast_to(place, (ROWS, LANES))
        of_slot = jnp.where(wide_place == first + (r16 // per_block).astype(f32), 1.0, 0.0)
        of_state = jnp.where(
            wide_place == first + lax.rem(r16, per_group).astype(f32), 1.0, 0.0
        )

        def mine(ref):
            out = jnp.zeros((ROWS, LANES), f32)
            for c in range(3):
                out = jnp.where(r16 // per_group == c, exact_dot(of_state, padded(ref[c])), out)
            return out

        half = mine(qvel_ref) + 0.5 * dt * mine(qacc_ref)
        qv[...] = half
        qp[...] = mine(qpos_ref) + dt * half

        pairs_s[...] = jnp.full(pairs_s.shape, -1, jnp.int32)
        for s in range(subs):
            pairs_s[2 * s : 2 * s + 2, 0:slots] = pairs_ref[s]
        earlier = jnp.where(wide_row < wide_lane, 1.0, 0.0)
        for s in range(subs):
            target = pairs_s[2 * s : 2 * s + 1].astype(f32)
            chosen = pairs_s[2 * s + 1 : 2 * s + 2].astype(f32)
            hit = exact_dot(of_slot, jnp.where(wide_row == chosen, 1.0, 0.0))
            order = exact_dot(hit, earlier)
            hit = jnp.where(order == lax.rem(r16, per_block).astype(f32), hit, 0.0)
            table = exact_dot(hit, jnp.where(column(target) * float(SL) == wide_lane, 1.0, 0.0))
            onehot[s] = table
            onehot_t[s] = padded(table).T
            live = jnp.sum(table, axis=1, keepdims=True)
            penalty[s] = jnp.broadcast_to(far * (1.0 - live), (ROWS, LANES))

    build_tables()
    three = wide_row < float(3 * ROWS)
    of_row = wide_row - float(ROWS) * jnp.floor(wide_row * (1.0 / ROWS))
    for i in range(3 * per_group):
        spread_row[i] = jnp.where(three & (of_row == float(i)), 1.0, 0.0).astype(bf16)
        one = jnp.where(wide_lane == float(i), 1.0, 0.0).astype(bf16)
        sum_column[i] = jnp.concatenate([one, one], axis=0)

    for a in range(3):
        for load in loads[a]:
            load.wait()

    def sweep(visit, after_edges, after_sides, after_layer):
        @pl.loop(0, nx, unroll=4)
        def _(x):
            for t in (0, tiles - 1):
                visit(x, t)

        after_edges()

        @pl.loop(0, 2, unroll=2)
        def _(i):
            for t in range(1, tiles - 1):
                visit(i * (nx - 1), t)
            after_layer(i * (nx - 1))

        after_sides()

        @pl.loop(1, nx - 1, unroll=3)
        def _(x):
            for t in range(1, tiles - 1):
                visit(x, t)
            after_layer(x)

    def send_edges(s):
        for k, (dx, dy) in enumerate(CORNERS):
            x = 2 if dx < 0 else nx + 1
            y = 8 if dy < 0 else ny + 7
            for c in range(3):
                for h in range(halves):
                    edges_c[s, k, c, h] = u_0[c, x, h, y : y + 1, :]
        for k, d in enumerate((1, -1)):
            @pl.when(exists(0, d))
            def _():
                copy_edge(s, k, d, 0).start()
        for k, (dx, dy) in enumerate(CORNERS):
            @pl.when(exists(dx, dy))
            def _():
                copy_corner(s, k, dx, dy).start()

    def send_far(s):
        send_sides(s, 1)
        for k, d in enumerate((1, -1)):
            @pl.when(exists(0, d))
            def _():
                copy_edge(s, k, d, 1).start()

    def send_sides(s, j):
        for k, d in enumerate((1, -1)):
            @pl.when(exists(d, 0))
            def _():
                copy_side(s, k, d, j).start()

    def nothing(*args):
        pass

    def first_step(x, t):
        rows = slice(8 * t, 8 * t + 8)
        advance(0, x, t, [
            [vel[c, x, rows, zs(h)] + 0.5 * dt * acc[c, x, rows, zs(h)] for c in range(3)]
            for h in range(halves)
        ])

    def greeted():
        count = groups - 1
        for dx, dy in SIDES + CORNERS:
            count = count + jnp.where(exists(dx, dy), 1, 0)
        pl.semaphore_wait(barrier, count)
        send_edges(0)

    sweep(first_step, greeted, lambda: send_sides(0, 0), nothing)
    send_far(0)

    def build_factors():
        above = [
            (word_bits(lambda e: e[i] == -1), word_bits(lambda e: e[i] == -2),
             word_bits(lambda e: e[i] == 1), word_bits(lambda e: e[i] == 2))
            for i in range(3)
        ]

        def allowed(at, size, i, w):
            one_down, two_down, one_up, two_up = (bits[w] for bits in above[i])
            keep = jnp.where(at < 1, 255 & ~one_down, 255)
            keep = keep & jnp.where(at < 2, 255 & ~two_down, 255)
            keep = keep & jnp.where(at > size - 2, 255 & ~one_up, 255)
            return keep & jnp.where(at > size - 3, 255 & ~two_up, 255)

        for h in range(halves):
            for t in range(tiles):
                for w in range(4):
                    at_y = me_y * ny + t * 8 + row8
                    at_z = lane + h * LANES
                    valid[h, t, w] = allowed(at_y, splits * ny, 1, w) & allowed(at_z, nz, 2, w)

        for load in loads[3]:
            load.wait()

        @pl.loop(0, nx, unroll=2)
        def _(x):
            ok_x = [allowed(me_x * nx + x, slabs * nx, 0, w) for w in range(4)]
            for t in range(tiles):
                rows = slice(8 * t, 8 * t + 8)
                words = [
                    [mask_ref[w, x, rows, zs(h)] & (valid[h, t, w] & ok_x[w]) for w in range(4)]
                    for h in range(halves)
                ]
                moved = {0: words}
                for by in (1, 2):
                    cols = [shifted([words[h][w] for h in range(halves)], by) for w in range(4)]
                    moved[by] = [[cols[w][h] for w in range(4)] for h in range(halves)]
                for h in range(halves):
                    for m, e in enumerate(HALF):
                        scale = bond_stiffness / square(e) * (2.0 if square(e) == 4 else 1.0)
                        minus = (-e[0], -e[1], -e[2])
                        for at, bond, frame in ((m, e, 0), (PAIRS + m, minus, e[2])):
                            n = NUMBER[bond]
                            bit = moved[frame][h][n // 8] & (1 << (n % 8))
                            factors[x, h, t, at] = jnp.where(bit != 0, scale, 0.0)

    stretch = math.sqrt(1.0 / (math.log(2.0) * contact_width))
    strength = contact_stiffness / stretch

    def contact(s):
        base = jnp.where(
            r16 // per_group == 0, (me_x * nx + mid_x).astype(f32),
            jnp.where(r16 // per_group == 1, (me_y * ny + mid_y).astype(f32), float(nz - SL)),
        )
        rel = (qp[...] - base) * stretch
        hi = rel.astype(bf16).astype(f32)
        mid = (rel - hi).astype(bf16).astype(f32)
        low = (rel - hi - mid).astype(bf16).astype(f32)
        split = padded(jnp.concatenate([hi, mid, low], axis=0)).T.astype(bf16)
        for i in range(3 * per_group):
            qb[i] = plain_dot(split, spread_row[i])
        for c in range(3):
            cols = []
            for t in range(tiles):
                col = zero_tile
                for x in range(nx):
                    tile = u_0[c, x + 2, top, 8 + 8 * t : 16 + 8 * t, :]
                    tile = pltpu.roll(tile, SL * x + SL, axis=1)
                    col = jnp.where(lane // SL == x, tile, col)
                cols.append(col)
            stack = []
            for z in range(SL):
                for col in cols:
                    col = pltpu.roll(col, (LANES - z) % LANES, axis=1) if z else col
                    stack.append(col + float(z) if c == 2 else col)
            table = exact_dot(onehot[s], jnp.concatenate(stack, axis=0).T * stretch)
            psel[c] = table + penalty[s] if c == 0 else table

        @pl.loop(0, per_group)
        def _(r):
            first = r * per_block
            points = [
                [jnp.broadcast_to(psel[c, pl.ds(first + j, 1), :], (8, LANES)) for c in range(3)]
                for j in range(per_block)
            ]
            on_points = [[zero_tile] * 3 for _ in range(per_block)]
            for i in range(PTS // 8):
                rows = slice(8 * i, 8 * i + 8)
                q = [qb[c * per_group + r, rows, :] for c in range(3)]
                pulls = [None] * 3
                for j in range(per_block):
                    d = [points[j][c] - q[c] for c in range(3)]
                    w = jnp.exp2(-(d[0] * d[0] + d[1] * d[1] + d[2] * d[2]))
                    for c in range(3):
                        pull = w * d[c]
                        pulls[c] = pull if pulls[c] is None else pulls[c] + pull
                        on_points[j][c] = on_points[j][c] + pull
                for c in range(3):
                    qb[c * per_group + r, rows, :] = pulls[c]
            for j in range(per_block):
                for c in range(3):
                    slot_rows[c, pl.ds(first + j, 1), :] = strength * jnp.sum(
                        on_points[j][c], axis=0, keepdims=True
                    )

        total = None
        for i in range(3 * per_group):
            hi = qb[i].astype(bf16)
            low = (qb[i] - hi.astype(f32)).astype(bf16)
            part = plain_dot(jnp.concatenate([hi, low], axis=1), sum_column[i])
            total = part if total is None else total + part
        rows = -strength * total.T[0:ROWS]
        part_send[s] = rows
        part_got[s, my_id] = rows
        for p, (fx, fy) in enumerate(partners):
            copy_part(s, p, fx, fy).start()

        for c in range(3):
            spread = exact_dot(onehot_t[s], slot_rows[c]).T
            for t in range(tiles):
                packed = zero_tile
                for z in range(SL):
                    tile = spread[z * ny + 8 * t : z * ny + 8 * t + 8]
                    tile = pltpu.roll(tile, z, axis=1) if z else tile
                    packed = jnp.where(lax.rem(lane, SL) == z, tile, packed)
                for x in range(nx):
                    tile = pltpu.roll(packed, LANES - SL - SL * x, axis=1) if x < nx else packed
                    pf[c, x, 8 * t : 8 * t + 8, :] = jnp.where(lane >= LANES - SL, tile, 0.0)

    def particle_force(s):
        for p, (fx, fy) in enumerate(partners):
            take_part(s, p, fx, fy).wait()
        total = part_got[s, 0] + part_got[s, 1] + part_got[s, 2] + part_got[s, 3]
        return inverse_mass * total

    slot_rows[...] = jnp.zeros(slot_rows.shape, f32)

    def put_side(s, k, j):
        d = (-1, 1)[k]
        x = 1 - j if d < 0 else nx + 2 + j
        for c in range(3):
            parts = [got_x[s, k, j, c, h] for h in range(halves)]
            if c == 0:
                parts = [p + float(d * nx) for p in parts]
            put(c, x, slice(8, 8 + ny), parts, j == 0)

    def put_corner(s, dx, dy):
        j = CORNERS.index((-dx, -dy))
        take_corner(s, j, dx, dy).wait_recv()
        x = 1 if dx < 0 else nx + 2
        y = 7 if dy < 0 else ny + 8
        for c in range(3):
            parts = [got_c[s, j, c, h] for h in range(halves)]
            if c == 0:
                parts = [p + float(dx * nx) for p in parts]
            if c == 1:
                parts = [p + float(dy * ny) for p in parts]
            put(c, x, slice(y, y + 1), parts)

    def put_edge(s, k, d, j):
        take_edge(s, k, d, j).wait_recv()
        y = 7 - j if d < 0 else ny + 8 + j
        for c in range(3):
            parts = [got_y[s, k, j, c, h] for h in range(halves)]
            if c == 1:
                parts = [p + float(d * ny) for p in parts]
            moved = shifted(parts, 1) if j == 0 else []
            if c == 2:
                moved = [p + 1.0 for p in moved]
            for ref, values in ((u_0, parts), (u_p, moved)):
                for h, p in enumerate(values):
                    for x in range(nx):
                        ref[c, x + 2, h, y : y + 1, :] = p[x : x + 1]

    def sent(s):
        for k, d in enumerate((1, -1)):
            @pl.when(exists(d, 0))
            def _():
                for j in range(2):
                    copy_side(s, k, d, j).wait_send()

            @pl.when(exists(0, d))
            def _():
                for j in range(2):
                    copy_edge(s, k, d, j).wait_send()
        for k, (dx, dy) in enumerate(CORNERS):
            @pl.when(exists(dx, dy))
            def _():
                copy_corner(s, k, dx, dy).wait_send()

    def substep(s):
        last = s == subs - 1

        @pl.when(s > 0)
        def _():
            half = qv[...] + dt * particle_force(s - 1)
            qv[...] = half
            qp[...] = qp[...] + dt * half

        @pl.when(last)
        def _():
            share(0, qp[...])
            for c in range(3):
                pltpu.make_async_copy(dsp.at[c, 0:nx, 0:ny], disp_out.at[c], out_sem.at[0, c]).start()

        contact(s)
        inner_lengths()

        @pl.when(s == 0)
        def _():
            build_factors()

        for k, d in enumerate((-1, 1)):
            @pl.when(exists(d, 0))
            def _():
                take_side(s, k, 0).wait_recv()
                put_side(s, k, 0)
        for dx, dy in CORNERS:
            @pl.when(exists(dx, dy))
            def _():
                put_corner(s, dx, dy)
        for k, d in enumerate((-1, 1)):
            @pl.when(exists(0, d))
            def _():
                put_edge(s, k, d, 0)

        @pl.loop(0, 2)
        def _(i):
            side_lengths(i * nx)

        edge_lengths()

        for k, d in enumerate((-1, 1)):
            @pl.when(exists(d, 0))
            def _():
                take_side(s, k, 1).wait_recv()
                put_side(s, k, 1)

            @pl.when(exists(0, d))
            def _():
                put_edge(s, k, d, 1)

        @pl.loop(0, 2)
        def _(i):
            far_lengths(i * nx)

        @pl.loop(0, nx, unroll=2)
        def _(x):
            for h in range(halves):
                for base in (0, ny):
                    lengths([y_two], x + 2, h, base)

        sent(s)

        @pl.when(s < subs - 1)
        def _():
            def visit(x, t):
                rows = slice(8 * t, 8 * t + 8)
                total = forces(x, t)
                advance(s + 1, x, t, [
                    [vel[c, x, rows, zs(h)] + dt * total[h][c] for c in range(3)]
                    for h in range(halves)
                ])

            sweep(visit, lambda: send_edges(s + 1), lambda: send_sides(s + 1, 0), nothing)
            send_far(s + 1)

        @pl.when(last)
        def _():
            share(1, qv[...] + 0.5 * dt * particle_force(s))

            def visit(x, t):
                rows = slice(8 * t, 8 * t + 8)
                total = forces(x, t)
                for h in range(halves):
                    for c in range(3):
                        vel[c, x, rows, zs(h)] = vel[c, x, rows, zs(h)] + 0.5 * dt * total[h][c]

            def leave(x):
                pltpu.make_async_copy(vel.at[:, x, 0:ny], vel_out.at[:, x], out_sem.at[1, x]).start()

            sweep(visit, nothing, nothing, leave)

    @pl.loop(0, subs)
    def _(s):
        substep(s)

    where = place_col[0:blocks]
    for i, dst in enumerate((pos_out, pvel_out)):
        @pl.loop(0, groups)
        def _(g):
            @pl.when(g != my_group)
            def _():
                take_group(i, g).wait()

        for c in range(3):
            out = None
            for k in range(0, groups * ROWS, LANES):
                rows = gathered[i, k // ROWS : (k + LANES) // ROWS].reshape(-1, LANES)
                pick = jnp.where(
                    where + float(c * per_group - k) == wide_lane[0:blocks], 1.0, 0.0
                )[:, 0 : rows.shape[0]]
                part = exact_dot(pick, rows)
                out = part if out is None else out + part
            ends[i, c] = out
        pltpu.make_async_copy(ends.at[i], dst, end_sem.at[i]).start()

    for c in range(3):
        pltpu.make_async_copy(dsp.at[c, 0:nx, 0:ny], disp_out.at[c], out_sem.at[0, c]).wait()

    @pl.loop(0, nx)
    def _(x):
        pltpu.make_async_copy(vel.at[:, x, 0:ny], vel_out.at[:, x], out_sem.at[1, x]).wait()

    for i, dst in enumerate((pos_out, pvel_out)):
        pltpu.make_async_copy(ends.at[i], dst, end_sem.at[i]).wait()


def finish_kernel(n, *refs):
    held, sem = refs[2 * n : 3 * n], refs[-1]
    loads = [pltpu.make_async_copy(refs[i], held[i], sem.at[0, i]) for i in range(n)]
    stores = [pltpu.make_async_copy(held[i], refs[n + i], sem.at[1, i]) for i in range(n)]
    for load in loads:
        load.start()
    for load, store in zip(loads, stores):
        load.wait()
        store.start()
    for store in stores:
        store.wait()


def finish(*arrays):
    anywhere = pl.BlockSpec(memory_space=pl.ANY)
    n = len(arrays)
    return pl.pallas_call(
        functools.partial(finish_kernel, n),
        out_shape=tuple(jax.ShapeDtypeStruct(a.shape, a.dtype) for a in arrays),
        in_specs=[anywhere] * n,
        out_specs=(anywhere,) * n,
        scratch_shapes=[pltpu.VMEM(a.shape, a.dtype) for a in arrays]
        + [pltpu.SemaphoreType.DMA((2, n))],
        compiler_params=pltpu.CompilerParams(vmem_limit_bytes=60 * 1024 * 1024),
    )(*arrays)


def per_device(
    slabs, splits,
    displacement, velocity, acceleration, bond_masks, proj_pos, proj_vel, proj_acc, contact_pairs
):
    _, nx, ny, nz = displacement.shape
    subs = contact_pairs.shape[0]
    blocks = proj_pos.shape[0]
    groups = (slabs // 2) * (splits // 2)
    per_group = blocks // groups
    halves = nz // LANES
    assert nx == SB_DEV and ny * SL == PTS and ny % 8 == 0
    assert per_group * 3 <= ROWS and blocks <= LANES and contact_pairs.shape[2] <= ROWS
    assert (groups * ROWS) % LANES == 0 or groups * ROWS < LANES

    dims = (subs, nx, ny, nz, slabs, splits, per_group, blocks)
    anywhere = pl.BlockSpec(memory_space=pl.ANY)
    padded = (3, nx + 5, halves, ny + 16, LANES)
    block = (3, nx + 1, ny + 8, nz)
    dma = pltpu.SemaphoreType.DMA
    scratch = [
        pltpu.VMEM((3, blocks, PTS), f32),
        pltpu.VMEM((3, blocks, PTS), f32),
        pltpu.VMEM((3, blocks, PTS), f32),
        pltpu.VMEM(contact_pairs.shape, jnp.int32),
        pltpu.VMEM((2, 3, blocks, PTS), f32),
        pltpu.VMEM(padded, f32),
        pltpu.VMEM(padded, f32),
        pltpu.VMEM((3, nx + 1, halves, ny + 8, LANES), f32),
        pltpu.VMEM(block, f32),
        pltpu.VMEM(block, f32),
        pltpu.VMEM(block, f32),
        pltpu.VMEM((4, nx, ny, nz), jnp.int32),
        pltpu.VMEM((halves, ny // 8, 4, 8, LANES), jnp.int32),
        pltpu.VMEM((nx, halves, ny // 8, 2 * PAIRS, 8, LANES), f32),
        pltpu.VMEM((PAIRS, nx + 3, halves * (ny + 16) + 8, LANES), f32),
        pltpu.VMEM((subs, 2, 2, 3, halves, nx, LANES), f32),
        pltpu.VMEM((subs, 4, 3, halves, 1, LANES), f32),
        pltpu.VMEM((subs, 2, 2, 3, halves, ny, LANES), f32),
        pltpu.VMEM((subs, 2, 2, 3, halves, nx, LANES), f32),
        pltpu.VMEM((subs, 4, 3, halves, 1, LANES), f32),
        pltpu.VMEM((3 * per_group, PTS, LANES), f32),
        pltpu.VMEM((3 * per_group, LANES, LANES), bf16),
        pltpu.VMEM((3 * per_group, 2 * LANES, LANES), bf16),
        pltpu.VMEM((3, ROWS, LANES), f32),
        pltpu.VMEM((3, LANES, LANES), f32),
        pltpu.VMEM((3, nx, ny, LANES), f32),
        pltpu.VMEM((8, LANES), jnp.int32),
        pltpu.VMEM((subs, ROWS, LANES), f32),
        pltpu.VMEM((subs, LANES, LANES), f32),
        pltpu.VMEM((subs, ROWS, LANES), f32),
        pltpu.VMEM((LANES, LANES), f32),
        pltpu.VMEM((ROWS, LANES), f32),
        pltpu.VMEM((ROWS, LANES), f32),
        pltpu.VMEM((subs, ROWS, LANES), f32),
        pltpu.VMEM((subs, 4, ROWS, LANES), f32),
        pltpu.VMEM((2, ROWS, LANES), f32),
        pltpu.VMEM((2, groups, ROWS, LANES), f32),
        dma((4, 2)), dma((4,)), dma((2, nx)), dma((2,)),
        dma((subs, 2, 2)), dma((subs, 2, 2)), dma((subs, 2, 2)), dma((subs, 2, 2)),
        dma((subs, 4)), dma((subs, 4)), dma((subs, 3)), dma((subs, 3)),
        dma((2, groups)), dma((2, groups)),
    ]
    moved, speed, points, point_speed = pl.pallas_call(
        functools.partial(kernel, dims),
        out_shape=(
            jax.ShapeDtypeStruct(displacement.shape, f32),
            jax.ShapeDtypeStruct(displacement.shape, f32),
            jax.ShapeDtypeStruct((3, blocks, PTS), f32),
            jax.ShapeDtypeStruct((3, blocks, PTS), f32),
        ),
        in_specs=[anywhere] * 8,
        out_specs=(anywhere,) * 4,
        scratch_shapes=scratch,
        compiler_params=pltpu.CompilerParams(
            collective_id=0, has_side_effects=True, vmem_limit_bytes=60 * 1024 * 1024
        ),
    )(
        displacement, velocity, acceleration, bond_masks,
        jnp.moveaxis(proj_pos, 1, 0), jnp.moveaxis(proj_vel, 1, 0), jnp.moveaxis(proj_acc, 1, 0),
        contact_pairs,
    )
    moved, speed, points, point_speed = finish(moved, speed, points, point_speed)
    return moved, speed, jnp.moveaxis(points, 0, 1), jnp.moveaxis(point_speed, 0, 1)


def solution(mesh):
    cells = P(None, "slab", "split", None)
    return jax.shard_map(
        functools.partial(per_device, mesh.shape["slab"], mesh.shape["split"]),
        mesh=mesh,
        in_specs=(cells, cells, cells, cells, P(), P(), P(), P(None, None, ("slab", "split"))),
        out_specs=(cells, cells, P(), P()),
        check_vma=False,
    )
```

```python
import functools
import math

import jax
import jax.numpy as jnp
from jax import lax
from jax.experimental import pallas as pl
from jax.experimental.pallas import tpu as pltpu
from jax.sharding import PartitionSpec as P

SL = 4
PTS = 128
SB_DEV = 8
LANES = 128
ROWS = 16

time_step = 0.25
bond_stiffness = 0.5
contact_stiffness = 0.05
contact_width = 8.0
inverse_mass = 0.5
tiny = 1e-30
far = 1e4
MESH = pl.DeviceIdType.MESH
f32 = jnp.float32
bf16 = jnp.bfloat16


def bond_offsets():
    listed = []
    for shift_x in (-2, -1, 0, 1, 2):
        for shift_y in (-2, -1, 0, 1, 2):
            for shift_z in (-2, -1, 0, 1, 2):
                squared = shift_x * shift_x + shift_y * shift_y + shift_z * shift_z
                if 0 < squared <= 4:
                    listed.append((shift_x, shift_y, shift_z))
    return listed


OFFSETS = bond_offsets()
NUMBER = {e: n for n, e in enumerate(OFFSETS)}
HALF = [(dx, dy, 1) for dx in (-1, 0, 1) for dy in (-1, 0, 1)] + [(0, 0, 2)] + [
    (1, 0, 0), (2, 0, 0), (0, 1, 0), (0, 2, 0), (1, 1, 0), (1, -1, 0)
]
INDEX = {e: m for m, e in enumerate(HALF)}
PAIRS = len(HALF)
CORNERS = [(-1, -1), (-1, 1), (1, -1), (1, 1)]
SIDES = [(-1, 0), (1, 0), (0, -1), (0, 1)]


def square(e):
    return e[0] * e[0] + e[1] * e[1] + e[2] * e[2]


def word_bits(test):
    words = [0, 0, 0, 0]
    for n, e in enumerate(OFFSETS):
        if test(e):
            words[n // 8] |= 1 << (n % 8)
    return words


def plain_dot(a, b):
    return lax.dot_general(a, b, (((1,), (0,)), ((), ())), preferred_element_type=f32)


def exact_dot(a, b):
    return lax.dot_general(
        a, b, (((1,), (0,)), ((), ())), precision=lax.Precision.HIGHEST, preferred_element_type=f32
    )


def kernel(
    dims,
    disp_hbm, vel_hbm, acc_hbm, mask_hbm, qpos_hbm, qvel_hbm, qacc_hbm, pairs_hbm,
    disp_out, vel_out, pos_out, pvel_out,
    qpos_ref, qvel_ref, qacc_ref, pairs_ref, ends,
    u_0, u_p, u_pp, dsp, vel, acc, mask_ref, valid, factors, rr, edges_y, edges_c,
    got_x, got_y, got_c, qb, spread_row, sum_column, psel, slot_rows, pf, pairs_s, onehot, onehot_t, penalty, place_col,
    qp, qv, part_send, part_got, fin, gathered,
    in_sem, small_sem, out_sem, end_sem, send_x, recv_x, send_y, recv_y, send_c, recv_c, send_p, recv_p, send_g, recv_g,
):
    subs, nx, ny, nz, slabs, splits, per_group, blocks = dims
    halves = nz // LANES
    tiles = ny // 8
    slots = pairs_ref.shape[2]
    per_block = slots // per_group
    top = halves - 1
    me_x = lax.axis_index("slab")
    me_y = lax.axis_index("split")
    mid_x, mid_y = nx // 2, ny // 2
    half_split = splits // 2
    groups = (slabs // 2) * half_split
    my_group = (me_x // 2) * half_split + me_y // 2
    my_x, my_y = lax.rem(me_x, 2), lax.rem(me_y, 2)
    my_id = my_x * 2 + my_y
    dt = time_step

    def exists(dx, dy):
        ok = None
        for d, me, n in ((dx, me_x, slabs), (dy, me_y, splits)):
            if d:
                cond = (me > 0) if d < 0 else (me < n - 1)
                ok = cond if ok is None else ok & cond
        return ok

    cut = nx // 2
    loads = [
        [
            pltpu.make_async_copy(
                src.at[:, i * cut : (i + 1) * cut], dst.at[:, i * cut : (i + 1) * cut, 0:ny],
                in_sem.at[a, i],
            )
            for i in range(2)
        ]
        for a, (src, dst) in enumerate(
            ((acc_hbm, acc), (vel_hbm, vel), (disp_hbm, dsp), (mask_hbm, mask_ref))
        )
    ]

    small = [
        pltpu.make_async_copy(src, dst, small_sem.at[i])
        for i, (src, dst) in enumerate((
            (qpos_hbm, qpos_ref), (qvel_hbm, qvel_ref), (qacc_hbm, qacc_ref), (pairs_hbm, pairs_ref)
        ))
    ]
    for load in small:
        load.start()
    for a in range(4):
        for load in loads[a]:
            load.start()

    barrier = pltpu.get_barrier_semaphore()

    def greet(x, y):
        pl.semaphore_signal(barrier, inc=1, device_id=(x, y), device_id_type=MESH)

    for dx, dy in SIDES + CORNERS:
        @pl.when(exists(dx, dy))
        def _():
            greet(me_x + dx, me_y + dy)

    def group_xy(g):
        return 2 * (g // half_split) + my_x, 2 * lax.rem(g, half_split) + my_y

    @pl.loop(0, groups)
    def _(g):
        @pl.when(g != my_group)
        def _():
            x, y = group_xy(g)
            greet(x, y)

    lane = lax.broadcasted_iota(jnp.int32, (8, LANES), 1)
    row8 = lax.broadcasted_iota(jnp.int32, (8, LANES), 0)
    zero_tile = jnp.zeros((8, LANES), f32)

    for ref in (u_0, u_p):
        for x in (0, 1, nx + 2, nx + 3):
            ref[:, x] = jnp.zeros(ref.shape[:1] + ref.shape[2:], f32)

        @pl.loop(2, nx + 2)
        def _(x):
            for c in range(3):
                for h in range(halves):
                    ref[c, x, h, 0:8, :] = zero_tile
                    ref[c, x, h, ny + 8 : ny + 16, :] = zero_tile

    def shifted(parts, by):
        rows = parts[0].shape[0]
        lanes = lax.broadcasted_iota(jnp.int32, (rows, LANES), 1)
        rolled = [pltpu.roll(p, (-by) % LANES, axis=1) for p in parts]
        out = []
        n = len(parts)
        for h in range(n):
            other = (h + 1) % n if by > 0 else (h - 1) % n
            edge = lanes >= LANES - by if by > 0 else lanes < -by
            out.append(jnp.where(edge, rolled[other], rolled[h]))
        return out

    def put(c, x, rows, parts, shifts=True):
        for h, p in enumerate(parts):
            u_0[c, x, h, rows, :] = p
        if shifts:
            for h, p in enumerate(shifted(parts, 1)):
                u_p[c, x, h, rows, :] = p + 1.0 if c == 2 else p

    def zs(h):
        return slice(h * LANES, (h + 1) * LANES)

    def advance(s, x, t, speeds):
        rows = slice(8 * t, 8 * t + 8)
        for c in range(3):
            parts = []
            for h in range(halves):
                half = speeds[h][c]
                vel[c, x, rows, zs(h)] = half
                moved = dsp[c, x, rows, zs(h)] + dt * half
                dsp[c, x, rows, zs(h)] = moved
                if c == 0:
                    moved = moved + (x - mid_x).astype(f32)
                elif c == 1:
                    moved = moved + (row8 + (8 * t - mid_y)).astype(f32)
                parts.append(moved)
            put(c, x + 2, slice(8 + 8 * t, 16 + 8 * t), parts)
            for h, p in enumerate(shifted(parts, 2)):
                u_pp[c, x, h, rows, :] = p + 2.0 if c == 2 else p
            for h, p in enumerate(parts):
                for j in range(2):
                    if t == 0:
                        edges_y[s, 0, j, c, h, pl.ds(x, 1), :] = p[j : j + 1]
                    if t == tiles - 1:
                        edges_y[s, 1, j, c, h, pl.ds(x, 1), :] = p[7 - j : 8 - j]

    def near_layer(d):
        return 0 if d < 0 else nx - 1

    def copy_side(s, k, d, j):
        layer = near_layer(d) - d * j
        return pltpu.make_async_remote_copy(
            src_ref=u_0.at[:, 2 + layer, :, 8 : 8 + ny, :], dst_ref=got_x.at[s, k, j],
            send_sem=send_x.at[s, k, j], recv_sem=recv_x.at[s, k, j],
            device_id=(me_x + d, me_y), device_id_type=MESH,
        )

    def take_side(s, k, j):
        d = (-1, 1)[k]
        return pltpu.make_async_remote_copy(
            src_ref=got_x.at[s, k, j], dst_ref=got_x.at[s, k, j],
            send_sem=send_x.at[s, k, j], recv_sem=recv_x.at[s, k, j],
            device_id=(me_x + d, me_y), device_id_type=MESH,
        )

    def copy_edge(s, k, d, j):
        return pltpu.make_async_remote_copy(
            src_ref=edges_y.at[s, 1 - k, j], dst_ref=got_y.at[s, k, j],
            send_sem=send_y.at[s, k, j], recv_sem=recv_y.at[s, k, j],
            device_id=(me_x, me_y + d), device_id_type=MESH,
        )

    def take_edge(s, k, d, j):
        return pltpu.make_async_remote_copy(
            src_ref=got_y.at[s, k, j], dst_ref=got_y.at[s, k, j], send_sem=send_y.at[s, k, j],
            recv_sem=recv_y.at[s, k, j], device_id=(me_x, me_y + d), device_id_type=MESH,
        )

    def copy_corner(s, k, dx, dy):
        return pltpu.make_async_remote_copy(
            src_ref=edges_c.at[s, k], dst_ref=got_c.at[s, k], send_sem=send_c.at[s, k],
            recv_sem=recv_c.at[s, k], device_id=(me_x + dx, me_y + dy), device_id_type=MESH,
        )

    def take_corner(s, j, dx, dy):
        return pltpu.make_async_remote_copy(
            src_ref=got_c.at[s, j], dst_ref=got_c.at[s, j], send_sem=send_c.at[s, j],
            recv_sem=recv_c.at[s, j], device_id=(me_x + dx, me_y + dy), device_id_type=MESH,
        )

    partners = ((0, 1), (1, 0), (1, 1))

    def flipped(fx, fy):
        return my_x + (1 - 2 * my_x) * fx, my_y + (1 - 2 * my_y) * fy

    def copy_part(s, p, fx, fy):
        ix, iy = flipped(fx, fy)
        return pltpu.make_async_remote_copy(
            src_ref=part_send.at[s], dst_ref=part_got.at[s, my_id], send_sem=send_p.at[s, p],
            recv_sem=recv_p.at[s, p], device_id=(me_x + ix - my_x, me_y + iy - my_y),
            device_id_type=MESH,
        )

    def take_part(s, p, fx, fy):
        ix, iy = flipped(fx, fy)
        return pltpu.make_async_remote_copy(
            src_ref=part_send.at[s], dst_ref=part_got.at[s, ix * 2 + iy], send_sem=send_p.at[s, p],
            recv_sem=recv_p.at[s, p], device_id=(me_x + ix - my_x, me_y + iy - my_y),
            device_id_type=MESH,
        )

    def copy_group(i, g):
        x, y = group_xy(g)
        return pltpu.make_async_remote_copy(
            src_ref=fin.at[i], dst_ref=gathered.at[i, my_group], send_sem=send_g.at[i, g],
            recv_sem=recv_g.at[i, my_group], device_id=(x, y), device_id_type=MESH,
        )

    def take_group(i, g):
        x, y = group_xy(g)
        return pltpu.make_async_remote_copy(
            src_ref=fin.at[i], dst_ref=gathered.at[i, g], send_sem=send_g.at[i, g],
            recv_sem=recv_g.at[i, g], device_id=(x, y), device_id_type=MESH,
        )

    def share(i, rows):
        fin[i] = rows
        gathered[i, my_group] = rows

        @pl.loop(0, groups)
        def _(g):
            @pl.when(g != my_group)
            def _():
                copy_group(i, g).start()

    def length(m, own, x, h, y):
        dx, dy, dz = HALF[m]
        if dz == 2:
            near = [u_pp[c, x - 2, h, pl.ds(y - 8, 8), :] for c in range(3)]
        else:
            ref = u_p if dz else u_0
            near = [ref[c, x + dx, h, pl.ds(y + dy, 8), :] for c in range(3)]
        d = [near[c] - own[c] for c in range(3)]
        q = d[0] * d[0] + d[1] * d[1] + d[2] * d[2]
        rr[m, x, pl.ds(h * (ny + 16) + y, 8), :] = (
            q * lax.rsqrt(jnp.maximum(q, tiny)) - math.sqrt(square(HALF[m]))
        )

    def lengths(ms, x, h, y):
        own = [u_0[c, x, h, pl.ds(y, 8), :] for c in range(3)]
        for m in ms:
            length(m, own, x, h, y)

    every = list(range(PAIRS))
    dx_up = [m for m in every if HALF[m][0] == 1]
    dx_down = [m for m in every if HALF[m][0] == -1]
    x_two = INDEX[(2, 0, 0)]
    y_two = INDEX[(0, 2, 0)]
    dy_up = [m for m in every if HALF[m][1] == 1]
    dy_down = [m for m in every if HALF[m][1] < 0]

    def inner_lengths():
        @pl.loop(0, nx, unroll=2)
        def _(x):
            for h in range(halves):
                for t in range(tiles):
                    lengths(every, x + 2, h, 8 + 8 * t)

    def side_lengths(base):
        for h in range(halves):
            for t in range(tiles):
                y = 8 + 8 * t
                lengths(dx_up, base + 1, h, y)
                lengths(dx_down, base + 2, h, y)

    def far_lengths(base):
        for h in range(halves):
            for t in range(tiles):
                lengths([x_two], base, h, 8 + 8 * t)
                lengths([x_two], base + 1, h, 8 + 8 * t)

    def edge_lengths():
        def one(ups, downs, x):
            for h in range(halves):
                for base in (0, ny):
                    if ups:
                        lengths(ups, x, h, base)
                    if downs:
                        lengths(downs, x, h, base + 8)

        @pl.loop(0, nx, unroll=2)
        def _(x):
            one(dy_up, dy_down, x + 2)

        one([m for m in dy_up if m in dx_up], [m for m in dy_down if m in dx_up], 1)
        one([m for m in dy_up if m in dx_down], [m for m in dy_down if m in dx_down], nx + 2)

    def plane_sums(c):
        sx = [c[i][0] + c[i][1] + c[i][2] for i in range(3)]
        fy = (c[0][2] + c[1][2] + c[2][2]) - (c[0][0] + c[1][0] + c[2][0])
        return [sx[2] - sx[0], fy, sx[0] + sx[1] + sx[2]]

    def forces(x, t):
        y = 8 + 8 * t
        rows = slice(8 * t, 8 * t + 8)
        total, back, back_two = [], [], []
        for h in range(halves):
            def forth(e):
                m = INDEX[e]
                at = h * (ny + 16) + y
                return rr[m, x + 2, at : at + 8, :] * factors[x, h, t, m]

            def behind(e):
                m = INDEX[e]
                at = h * (ny + 16) + y - e[1]
                return rr[m, x + 2 - e[0], at : at + 8, :] * factors[x, h, t, PAIRS + m]

            up = plane_sums([[forth((dx, dy, 1)) for dy in (-1, 0, 1)] for dx in (-1, 0, 1)])
            down = plane_sums([[behind((dx, dy, 1)) for dy in (-1, 0, 1)] for dx in (-1, 0, 1)])

            def net(e):
                return forth(e) - behind(e)

            a, b = net((1, 1, 0)), net((1, -1, 0))
            fx = (a + b) + (net((1, 0, 0)) + net((2, 0, 0)))
            fy = (a - b) + (net((0, 1, 0)) + net((0, 2, 0)))
            total.append([up[0] + fx, up[1] + fy, up[2] + forth((0, 0, 2))])
            back.append(down)
            back_two.append(behind((0, 0, 2)))
        for c in range(3):
            for h, p in enumerate(shifted([back[h][c] for h in range(halves)], -1)):
                total[h][c] = total[h][c] - p
        for h, p in enumerate(shifted(back_two, -2)):
            total[h][2] = total[h][2] - p
        for c in range(3):
            total[top][c] = total[top][c] + pf[c, x, rows, :]
        return total

    wide_lane = lax.broadcasted_iota(jnp.int32, (LANES, LANES), 1).astype(f32)
    wide_row = lax.broadcasted_iota(jnp.int32, (LANES, LANES), 0).astype(f32)
    r16 = lax.broadcasted_iota(jnp.int32, (ROWS, LANES), 0)

    def padded(a):
        n = a.shape[0]
        return a if n == LANES else jnp.concatenate([a, jnp.zeros((LANES - n, LANES), f32)], axis=0)

    def column(row):
        return jnp.broadcast_to(row, (LANES, LANES)).T

    def build_tables():
        for load in small:
            load.wait()
        where = []
        for c, (size, most) in enumerate(((2 * nx, slabs // 2), (2 * ny, half_split))):
            sums = jnp.sum(padded(qpos_ref[c]).T, axis=0, keepdims=True)
            cell = jnp.floor((sums * (1.0 / PTS) + 0.5) * (1.0 / size))
            where.append(jnp.clip(cell, 0.0, float(most - 1)))
        group = where[0] * float(half_split) + where[1]
        same = (column(group) == group) & (wide_row < wide_lane)
        rank = jnp.sum(jnp.where(same, 1.0, 0.0), axis=0, keepdims=True)
        place = group * float(ROWS) + jnp.minimum(rank, float(per_group - 1))
        place = jnp.where(wide_lane[0:1] < float(blocks), place, -1e6)
        place_col[...] = column(place)
        first = (my_group * ROWS).astype(f32)
        wide_place = jnp.broadcast_to(place, (ROWS, LANES))
        of_slot = jnp.where(wide_place == first + (r16 // per_block).astype(f32), 1.0, 0.0)
        of_state = jnp.where(
            wide_place == first + lax.rem(r16, per_group).astype(f32), 1.0, 0.0
        )

        def mine(ref):
            out = jnp.zeros((ROWS, LANES), f32)
            for c in range(3):
                out = jnp.where(r16 // per_group == c, exact_dot(of_state, padded(ref[c])), out)
            return out

        half = mine(qvel_ref) + 0.5 * dt * mine(qacc_ref)
        qv[...] = half
        qp[...] = mine(qpos_ref) + dt * half

        pairs_s[...] = jnp.full(pairs_s.shape, -1, jnp.int32)
        for s in range(subs):
            pairs_s[2 * s : 2 * s + 2, 0:slots] = pairs_ref[s]
        earlier = jnp.where(wide_row < wide_lane, 1.0, 0.0)
        for s in range(subs):
            target = pairs_s[2 * s : 2 * s + 1].astype(f32)
            chosen = pairs_s[2 * s + 1 : 2 * s + 2].astype(f32)
            hit = exact_dot(of_slot, jnp.where(wide_row == chosen, 1.0, 0.0))
            order = exact_dot(hit, earlier)
            hit = jnp.where(order == lax.rem(r16, per_block).astype(f32), hit, 0.0)
            table = exact_dot(hit, jnp.where(column(target) * float(SL) == wide_lane, 1.0, 0.0))
            onehot[s] = table
            onehot_t[s] = padded(table).T[0 : SL * nx]
            live = jnp.sum(table, axis=1, keepdims=True)
            penalty[s] = jnp.broadcast_to(far * (1.0 - live), (ROWS, LANES))

    build_tables()
    three = wide_row < float(3 * ROWS)
    of_row = wide_row - float(ROWS) * jnp.floor(wide_row * (1.0 / ROWS))
    for i in range(3 * per_group):
        spread_row[i] = jnp.where(three & (of_row == float(i)), 1.0, 0.0).astype(bf16)
        one = jnp.where(wide_lane == float(i), 1.0, 0.0).astype(bf16)
        sum_column[i] = jnp.concatenate([one, one], axis=0)

    for a in range(3):
        for load in loads[a]:
            load.wait()

    def sweep(visit, after_edges, after_sides, after_layer):
        @pl.loop(0, nx, unroll=4)
        def _(x):
            for t in (0, tiles - 1):
                visit(x, t)

        after_edges()

        @pl.loop(0, 2, unroll=2)
        def _(i):
            for t in range(1, tiles - 1):
                visit(i * (nx - 1), t)
            after_layer(i * (nx - 1))

        after_sides()

        @pl.loop(1, nx - 1, unroll=3)
        def _(x):
            for t in range(1, tiles - 1):
                visit(x, t)
            after_layer(x)

    def send_edges(s):
        for k, (dx, dy) in enumerate(CORNERS):
            x = 2 if dx < 0 else nx + 1
            y = 8 if dy < 0 else ny + 7
            for c in range(3):
                for h in range(halves):
                    edges_c[s, k, c, h] = u_0[c, x, h, y : y + 1, :]
        for k, d in enumerate((1, -1)):
            @pl.when(exists(0, d))
            def _():
                copy_edge(s, k, d, 0).start()
        for k, (dx, dy) in enumerate(CORNERS):
            @pl.when(exists(dx, dy))
            def _():
                copy_corner(s, k, dx, dy).start()

    def send_far(s):
        send_sides(s, 1)
        for k, d in enumerate((1, -1)):
            @pl.when(exists(0, d))
            def _():
                copy_edge(s, k, d, 1).start()

    def send_sides(s, j):
        for k, d in enumerate((1, -1)):
            @pl.when(exists(d, 0))
            def _():
                copy_side(s, k, d, j).start()

    def nothing(*args):
        pass

    def first_step(x, t):
        rows = slice(8 * t, 8 * t + 8)
        advance(0, x, t, [
            [vel[c, x, rows, zs(h)] + 0.5 * dt * acc[c, x, rows, zs(h)] for c in range(3)]
            for h in range(halves)
        ])

    def greeted():
        count = groups - 1
        for dx, dy in SIDES + CORNERS:
            count = count + jnp.where(exists(dx, dy), 1, 0)
        pl.semaphore_wait(barrier, count)
        send_edges(0)

    sweep(first_step, greeted, lambda: send_sides(0, 0), nothing)
    send_far(0)

    def build_factors():
        above = [
            (word_bits(lambda e: e[i] == -1), word_bits(lambda e: e[i] == -2),
             word_bits(lambda e: e[i] == 1), word_bits(lambda e: e[i] == 2))
            for i in range(3)
        ]

        def allowed(at, size, i, w):
            one_down, two_down, one_up, two_up = (bits[w] for bits in above[i])
            keep = jnp.where(at < 1, 255 & ~one_down, 255)
            keep = keep & jnp.where(at < 2, 255 & ~two_down, 255)
            keep = keep & jnp.where(at > size - 2, 255 & ~one_up, 255)
            return keep & jnp.where(at > size - 3, 255 & ~two_up, 255)

        for h in range(halves):
            for t in range(tiles):
                for w in range(4):
                    at_y = me_y * ny + t * 8 + row8
                    at_z = lane + h * LANES
                    valid[h, t, w] = allowed(at_y, splits * ny, 1, w) & allowed(at_z, nz, 2, w)

        for load in loads[3]:
            load.wait()

        @pl.loop(0, nx, unroll=2)
        def _(x):
            ok_x = [allowed(me_x * nx + x, slabs * nx, 0, w) for w in range(4)]
            for t in range(tiles):
                rows = slice(8 * t, 8 * t + 8)
                words = [
                    [mask_ref[w, x, rows, zs(h)] & (valid[h, t, w] & ok_x[w]) for w in range(4)]
                    for h in range(halves)
                ]
                moved = {0: words}
                for by in (1, 2):
                    cols = [shifted([words[h][w] for h in range(halves)], by) for w in range(4)]
                    moved[by] = [[cols[w][h] for w in range(4)] for h in range(halves)]
                for h in range(halves):
                    for m, e in enumerate(HALF):
                        scale = bond_stiffness / square(e) * (2.0 if square(e) == 4 else 1.0)
                        minus = (-e[0], -e[1], -e[2])
                        for at, bond, frame in ((m, e, 0), (PAIRS + m, minus, e[2])):
                            n = NUMBER[bond]
                            bit = moved[frame][h][n // 8] & (1 << (n % 8))
                            factors[x, h, t, at] = jnp.where(bit != 0, scale, 0.0)

    stretch = math.sqrt(1.0 / (math.log(2.0) * contact_width))
    strength = contact_stiffness / stretch

    def contact(s):
        base = jnp.where(
            r16 // per_group == 0, (me_x * nx + mid_x).astype(f32),
            jnp.where(r16 // per_group == 1, (me_y * ny + mid_y).astype(f32), float(nz - SL)),
        )
        rel = (qp[...] - base) * stretch
        hi = rel.astype(bf16).astype(f32)
        mid = (rel - hi).astype(bf16).astype(f32)
        low = (rel - hi - mid).astype(bf16).astype(f32)
        split = padded(jnp.concatenate([hi, mid, low], axis=0)).T.astype(bf16)
        for i in range(3 * per_group):
            qb[i] = plain_dot(split, spread_row[i])
        for c in range(3):
            cols = []
            for t in range(tiles):
                col = zero_tile
                for x in range(nx):
                    tile = u_0[c, x + 2, top, 8 + 8 * t : 16 + 8 * t, :]
                    tile = pltpu.roll(tile, SL * x + SL, axis=1)
                    col = jnp.where(lane // SL == x, tile, col)
                cols.append(col)
            stack = []
            for z in range(SL):
                for col in cols:
                    col = pltpu.roll(col, (LANES - z) % LANES, axis=1) if z else col
                    stack.append(col + float(z) if c == 2 else col)
            places = jnp.concatenate(stack, axis=0).T[0 : SL * nx] * stretch
            table = exact_dot(onehot[s, :, 0 : SL * nx], places)
            psel[c] = table + penalty[s] if c == 0 else table

        @pl.loop(0, per_group)
        def _(r):
            first = r * per_block
            points = [
                [jnp.broadcast_to(psel[c, pl.ds(first + j, 1), :], (8, LANES)) for c in range(3)]
                for j in range(per_block)
            ]
            on_points = [[zero_tile] * 3 for _ in range(per_block)]
            for i in range(PTS // 8):
                rows = slice(8 * i, 8 * i + 8)
                q = [qb[c * per_group + r, rows, :] for c in range(3)]
                pulls = [None] * 3
                for j in range(per_block):
                    d = [points[j][c] - q[c] for c in range(3)]
                    w = jnp.exp2(-(d[0] * d[0] + d[1] * d[1] + d[2] * d[2]))
                    for c in range(3):
                        pull = w * d[c]
                        pulls[c] = pull if pulls[c] is None else pulls[c] + pull
                        on_points[j][c] = on_points[j][c] + pull
                for c in range(3):
                    qb[c * per_group + r, rows, :] = pulls[c]
            for j in range(per_block):
                for c in range(3):
                    slot_rows[c, pl.ds(first + j, 1), :] = strength * jnp.sum(
                        on_points[j][c], axis=0, keepdims=True
                    )

        total = None
        for i in range(3 * per_group):
            hi = qb[i].astype(bf16)
            low = (qb[i] - hi.astype(f32)).astype(bf16)
            part = plain_dot(jnp.concatenate([hi, low], axis=1), sum_column[i])
            total = part if total is None else total + part
        rows = -strength * total.T[0:ROWS]
        part_send[s] = rows
        part_got[s, my_id] = rows
        for c in range(3):
            spread = padded(exact_dot(onehot_t[s], slot_rows[c])).T
            for t in range(tiles):
                packed = zero_tile
                for z in range(SL):
                    tile = spread[z * ny + 8 * t : z * ny + 8 * t + 8]
                    tile = pltpu.roll(tile, z, axis=1) if z else tile
                    packed = jnp.where(lax.rem(lane, SL) == z, tile, packed)
                for x in range(nx):
                    tile = pltpu.roll(packed, LANES - SL - SL * x, axis=1) if x < nx else packed
                    pf[c, x, 8 * t : 8 * t + 8, :] = jnp.where(lane >= LANES - SL, tile, 0.0)
        for p, (fx, fy) in enumerate(partners):
            copy_part(s, p, fx, fy).start()

    def particle_force(s):
        for p, (fx, fy) in enumerate(partners):
            take_part(s, p, fx, fy).wait()
        total = part_got[s, 0] + part_got[s, 1] + part_got[s, 2] + part_got[s, 3]
        return inverse_mass * total

    slot_rows[...] = jnp.zeros(slot_rows.shape, f32)

    def put_side(s, k, j):
        d = (-1, 1)[k]
        x = 1 - j if d < 0 else nx + 2 + j
        for c in range(3):
            parts = [got_x[s, k, j, c, h] for h in range(halves)]
            if c == 0:
                parts = [p + float(d * nx) for p in parts]
            put(c, x, slice(8, 8 + ny), parts, j == 0)

    def put_corner(s, dx, dy):
        j = CORNERS.index((-dx, -dy))
        take_corner(s, j, dx, dy).wait_recv()
        x = 1 if dx < 0 else nx + 2
        y = 7 if dy < 0 else ny + 8
        for c in range(3):
            parts = [got_c[s, j, c, h] for h in range(halves)]
            if c == 0:
                parts = [p + float(dx * nx) for p in parts]
            if c == 1:
                parts = [p + float(dy * ny) for p in parts]
            put(c, x, slice(y, y + 1), parts)

    def put_edge(s, k, d, j):
        take_edge(s, k, d, j).wait_recv()
        y = 7 - j if d < 0 else ny + 8 + j
        for c in range(3):
            parts = [got_y[s, k, j, c, h] for h in range(halves)]
            if c == 1:
                parts = [p + float(d * ny) for p in parts]
            moved = shifted(parts, 1) if j == 0 else []
            if c == 2:
                moved = [p + 1.0 for p in moved]
            for ref, values in ((u_0, parts), (u_p, moved)):
                for h, p in enumerate(values):
                    for x in range(nx):
                        ref[c, x + 2, h, y : y + 1, :] = p[x : x + 1]

    def sent(s):
        for k, d in enumerate((1, -1)):
            @pl.when(exists(d, 0))
            def _():
                for j in range(2):
                    copy_side(s, k, d, j).wait_send()

            @pl.when(exists(0, d))
            def _():
                for j in range(2):
                    copy_edge(s, k, d, j).wait_send()
        for k, (dx, dy) in enumerate(CORNERS):
            @pl.when(exists(dx, dy))
            def _():
                copy_corner(s, k, dx, dy).wait_send()

    def substep(s):
        last = s == subs - 1

        @pl.when(s > 0)
        def _():
            half = qv[...] + dt * particle_force(s - 1)
            qv[...] = half
            qp[...] = qp[...] + dt * half

        @pl.when(last)
        def _():
            share(0, qp[...])
            for c in range(3):
                pltpu.make_async_copy(dsp.at[c, 0:nx, 0:ny], disp_out.at[c], out_sem.at[0, c]).start()

        contact(s)
        inner_lengths()

        @pl.when(s == 0)
        def _():
            build_factors()

        for k, d in enumerate((-1, 1)):
            @pl.when(exists(d, 0))
            def _():
                take_side(s, k, 0).wait_recv()
                put_side(s, k, 0)
        for dx, dy in CORNERS:
            @pl.when(exists(dx, dy))
            def _():
                put_corner(s, dx, dy)
        for k, d in enumerate((-1, 1)):
            @pl.when(exists(0, d))
            def _():
                put_edge(s, k, d, 0)

        @pl.loop(0, 2)
        def _(i):
            side_lengths(i * nx)

        edge_lengths()

        for k, d in enumerate((-1, 1)):
            @pl.when(exists(d, 0))
            def _():
                take_side(s, k, 1).wait_recv()
                put_side(s, k, 1)

            @pl.when(exists(0, d))
            def _():
                put_edge(s, k, d, 1)

        @pl.loop(0, 2)
        def _(i):
            far_lengths(i * nx)

        @pl.loop(0, nx, unroll=2)
        def _(x):
            for h in range(halves):
                for base in (0, ny):
                    lengths([y_two], x + 2, h, base)

        sent(s)

        @pl.when(s < subs - 1)
        def _():
            def visit(x, t):
                rows = slice(8 * t, 8 * t + 8)
                total = forces(x, t)
                advance(s + 1, x, t, [
                    [vel[c, x, rows, zs(h)] + dt * total[h][c] for c in range(3)]
                    for h in range(halves)
                ])

            sweep(visit, lambda: send_edges(s + 1), lambda: send_sides(s + 1, 0), nothing)
            send_far(s + 1)

        @pl.when(last)
        def _():
            share(1, qv[...] + 0.5 * dt * particle_force(s))

            def visit(x, t):
                rows = slice(8 * t, 8 * t + 8)
                total = forces(x, t)
                for h in range(halves):
                    for c in range(3):
                        vel[c, x, rows, zs(h)] = vel[c, x, rows, zs(h)] + 0.5 * dt * total[h][c]

            def leave(x):
                pltpu.make_async_copy(vel.at[:, x, 0:ny], vel_out.at[:, x], out_sem.at[1, x]).start()

            sweep(visit, nothing, nothing, leave)

    @pl.loop(0, subs)
    def _(s):
        substep(s)

    where = place_col[0:blocks]
    for i, dst in enumerate((pos_out, pvel_out)):
        @pl.loop(0, groups)
        def _(g):
            @pl.when(g != my_group)
            def _():
                take_group(i, g).wait()

        for c in range(3):
            out = None
            for k in range(0, groups * ROWS, LANES):
                rows = gathered[i, k // ROWS : (k + LANES) // ROWS].reshape(-1, LANES)
                pick = jnp.where(
                    where + float(c * per_group - k) == wide_lane[0:blocks], 1.0, 0.0
                )[:, 0 : rows.shape[0]]
                part = exact_dot(pick, rows)
                out = part if out is None else out + part
            ends[i, c] = out
        pltpu.make_async_copy(ends.at[i], dst, end_sem.at[i]).start()

    for c in range(3):
        pltpu.make_async_copy(dsp.at[c, 0:nx, 0:ny], disp_out.at[c], out_sem.at[0, c]).wait()

    @pl.loop(0, nx)
    def _(x):
        pltpu.make_async_copy(vel.at[:, x, 0:ny], vel_out.at[:, x], out_sem.at[1, x]).wait()

    for i, dst in enumerate((pos_out, pvel_out)):
        pltpu.make_async_copy(ends.at[i], dst, end_sem.at[i]).wait()


def finish_kernel(n, *refs):
    copies = [pltpu.make_async_copy(refs[i], refs[n + i], refs[-1].at[i]) for i in range(n)]
    for copy in copies:
        copy.start()
    for copy in copies:
        copy.wait()


def finish(*arrays):
    anywhere = pl.BlockSpec(memory_space=pl.ANY)
    n = len(arrays)
    return pl.pallas_call(
        functools.partial(finish_kernel, n),
        out_shape=tuple(jax.ShapeDtypeStruct(a.shape, a.dtype) for a in arrays),
        in_specs=[anywhere] * n,
        out_specs=(anywhere,) * n,
        scratch_shapes=[pltpu.SemaphoreType.DMA((n,))],
        compiler_params=pltpu.CompilerParams(vmem_limit_bytes=4 * 1024 * 1024),
    )(*arrays)


def per_device(
    slabs, splits,
    displacement, velocity, acceleration, bond_masks, proj_pos, proj_vel, proj_acc, contact_pairs
):
    _, nx, ny, nz = displacement.shape
    subs = contact_pairs.shape[0]
    blocks = proj_pos.shape[0]
    groups = (slabs // 2) * (splits // 2)
    per_group = blocks // groups
    halves = nz // LANES
    assert nx == SB_DEV and ny * SL == PTS and ny % 8 == 0
    assert per_group * 3 <= ROWS and blocks <= LANES and contact_pairs.shape[2] <= ROWS
    assert (groups * ROWS) % LANES == 0 or groups * ROWS < LANES

    dims = (subs, nx, ny, nz, slabs, splits, per_group, blocks)
    anywhere = pl.BlockSpec(memory_space=pl.ANY)
    padded = (3, nx + 5, halves, ny + 16, LANES)
    block = (3, nx + 1, ny + 8, nz)
    dma = pltpu.SemaphoreType.DMA
    scratch = [
        pltpu.VMEM((3, blocks, PTS), f32),
        pltpu.VMEM((3, blocks, PTS), f32),
        pltpu.VMEM((3, blocks, PTS), f32),
        pltpu.VMEM(contact_pairs.shape, jnp.int32),
        pltpu.VMEM((2, 3, blocks, PTS), f32),
        pltpu.VMEM(padded, f32),
        pltpu.VMEM(padded, f32),
        pltpu.VMEM((3, nx + 1, halves, ny + 8, LANES), f32),
        pltpu.VMEM(block, f32),
        pltpu.VMEM(block, f32),
        pltpu.VMEM(block, f32),
        pltpu.VMEM((4, nx, ny, nz), jnp.int32),
        pltpu.VMEM((halves, ny // 8, 4, 8, LANES), jnp.int32),
        pltpu.VMEM((nx, halves, ny // 8, 2 * PAIRS, 8, LANES), f32),
        pltpu.VMEM((PAIRS, nx + 3, halves * (ny + 16) + 8, LANES), f32),
        pltpu.VMEM((subs, 2, 2, 3, halves, nx, LANES), f32),
        pltpu.VMEM((subs, 4, 3, halves, 1, LANES), f32),
        pltpu.VMEM((subs, 2, 2, 3, halves, ny, LANES), f32),
        pltpu.VMEM((subs, 2, 2, 3, halves, nx, LANES), f32),
        pltpu.VMEM((subs, 4, 3, halves, 1, LANES), f32),
        pltpu.VMEM((3 * per_group, PTS, LANES), f32),
        pltpu.VMEM((3 * per_group, LANES, LANES), bf16),
        pltpu.VMEM((3 * per_group, 2 * LANES, LANES), bf16),
        pltpu.VMEM((3, ROWS, LANES), f32),
        pltpu.VMEM((3, LANES, LANES), f32),
        pltpu.VMEM((3, nx, ny, LANES), f32),
        pltpu.VMEM((8, LANES), jnp.int32),
        pltpu.VMEM((subs, ROWS, LANES), f32),
        pltpu.VMEM((subs, SL * nx, LANES), f32),
        pltpu.VMEM((subs, ROWS, LANES), f32),
        pltpu.VMEM((LANES, LANES), f32),
        pltpu.VMEM((ROWS, LANES), f32),
        pltpu.VMEM((ROWS, LANES), f32),
        pltpu.VMEM((subs, ROWS, LANES), f32),
        pltpu.VMEM((subs, 4, ROWS, LANES), f32),
        pltpu.VMEM((2, ROWS, LANES), f32),
        pltpu.VMEM((2, groups, ROWS, LANES), f32),
        dma((4, 2)), dma((4,)), dma((2, nx)), dma((2,)),
        dma((subs, 2, 2)), dma((subs, 2, 2)), dma((subs, 2, 2)), dma((subs, 2, 2)),
        dma((subs, 4)), dma((subs, 4)), dma((subs, 3)), dma((subs, 3)),
        dma((2, groups)), dma((2, groups)),
    ]
    moved, speed, points, point_speed = pl.pallas_call(
        functools.partial(kernel, dims),
        out_shape=(
            pltpu.VMEM(displacement.shape, f32),
            pltpu.VMEM(displacement.shape, f32),
            pltpu.VMEM((3, blocks, PTS), f32),
            pltpu.VMEM((3, blocks, PTS), f32),
        ),
        in_specs=[anywhere] * 8,
        out_specs=(anywhere,) * 4,
        scratch_shapes=scratch,
        compiler_params=pltpu.CompilerParams(
            collective_id=0, has_side_effects=True, vmem_limit_bytes=58 * 1024 * 1024
        ),
    )(
        displacement, velocity, acceleration, bond_masks,
        jnp.moveaxis(proj_pos, 1, 0), jnp.moveaxis(proj_vel, 1, 0), jnp.moveaxis(proj_acc, 1, 0),
        contact_pairs,
    )
    moved, speed, points, point_speed = finish(moved, speed, points, point_speed)
    return moved, speed, jnp.moveaxis(points, 0, 1), jnp.moveaxis(point_speed, 0, 1)


def solution(mesh):
    cells = P(None, "slab", "split", None)
    return jax.shard_map(
        functools.partial(per_device, mesh.shape["slab"], mesh.shape["split"]),
        mesh=mesh,
        in_specs=(cells, cells, cells, cells, P(), P(), P(), P(None, None, ("slab", "split"))),
        out_specs=(cells, cells, P(), P()),
        check_vma=False,
    )
```

```python
import functools
import math

import jax
import jax.numpy as jnp
from jax import lax
from jax.experimental import pallas as pl
from jax.experimental.pallas import tpu as pltpu
from jax.sharding import PartitionSpec as P

SL = 4
PTS = 128
SB_DEV = 8
LANES = 128
ROWS = 16

time_step = 0.25
bond_stiffness = 0.5
contact_stiffness = 0.05
contact_width = 8.0
inverse_mass = 0.5
tiny = 1e-30
far = 1e4
MESH = pl.DeviceIdType.MESH
f32 = jnp.float32
bf16 = jnp.bfloat16


def bond_offsets():
    listed = []
    for shift_x in (-2, -1, 0, 1, 2):
        for shift_y in (-2, -1, 0, 1, 2):
            for shift_z in (-2, -1, 0, 1, 2):
                squared = shift_x * shift_x + shift_y * shift_y + shift_z * shift_z
                if 0 < squared <= 4:
                    listed.append((shift_x, shift_y, shift_z))
    return listed


OFFSETS = bond_offsets()
NUMBER = {e: n for n, e in enumerate(OFFSETS)}
HALF = [(dx, dy, 1) for dx in (-1, 0, 1) for dy in (-1, 0, 1)] + [(0, 0, 2)] + [
    (1, 0, 0), (2, 0, 0), (0, 1, 0), (0, 2, 0), (1, 1, 0), (1, -1, 0)
]
INDEX = {e: m for m, e in enumerate(HALF)}
PAIRS = len(HALF)
CORNERS = [(-1, -1), (-1, 1), (1, -1), (1, 1)]
SIDES = [(-1, 0), (1, 0), (0, -1), (0, 1)]


def square(e):
    return e[0] * e[0] + e[1] * e[1] + e[2] * e[2]


def word_bits(test):
    words = [0, 0, 0, 0]
    for n, e in enumerate(OFFSETS):
        if test(e):
            words[n // 8] |= 1 << (n % 8)
    return words


def plain_dot(a, b):
    return lax.dot_general(a, b, (((1,), (0,)), ((), ())), preferred_element_type=f32)


def exact_dot(a, b):
    return lax.dot_general(
        a, b, (((1,), (0,)), ((), ())), precision=lax.Precision.HIGHEST, preferred_element_type=f32
    )


def kernel(
    dims,
    disp_hbm, vel_hbm, acc_hbm, mask_hbm, qpos_hbm, qvel_hbm, qacc_hbm, pairs_hbm,
    disp_out, vel_out, pos_out, pvel_out,
    qpos_ref, qvel_ref, qacc_ref, pairs_ref, ends,
    u_0, u_p, u_pp, dsp, vel, acc, mask_ref, valid, factors, rr, edges_y, edges_c,
    got_x, got_y, got_c, qb, spread_row, sum_column, psel, slot_rows, pf, pairs_s, onehot, onehot_t, penalty, place_col,
    qp, qv, part_send, part_got, fin, gathered,
    in_sem, small_sem, out_sem, end_sem, send_x, recv_x, send_y, recv_y, send_c, recv_c, send_p, recv_p, send_g, recv_g,
):
    subs, nx, ny, nz, slabs, splits, per_group, blocks = dims
    halves = nz // LANES
    tiles = ny // 8
    slots = pairs_ref.shape[2]
    per_block = slots // per_group
    top = halves - 1
    me_x = lax.axis_index("slab")
    me_y = lax.axis_index("split")
    mid_x, mid_y = nx // 2, ny // 2
    half_split = splits // 2
    groups = (slabs // 2) * half_split
    my_group = (me_x // 2) * half_split + me_y // 2
    my_x, my_y = lax.rem(me_x, 2), lax.rem(me_y, 2)
    my_id = my_x * 2 + my_y
    dt = time_step

    def exists(dx, dy):
        ok = None
        for d, me, n in ((dx, me_x, slabs), (dy, me_y, splits)):
            if d:
                cond = (me > 0) if d < 0 else (me < n - 1)
                ok = cond if ok is None else ok & cond
        return ok

    cut = nx // 2
    loads = [
        [
            pltpu.make_async_copy(
                src.at[:, i * cut : (i + 1) * cut], dst.at[:, i * cut : (i + 1) * cut, 0:ny],
                in_sem.at[a, i],
            )
            for i in range(2)
        ]
        for a, (src, dst) in enumerate(
            ((acc_hbm, acc), (vel_hbm, vel), (disp_hbm, dsp), (mask_hbm, mask_ref))
        )
    ]

    small = [
        pltpu.make_async_copy(src, dst, small_sem.at[i])
        for i, (src, dst) in enumerate((
            (qpos_hbm, qpos_ref), (qvel_hbm, qvel_ref), (qacc_hbm, qacc_ref), (pairs_hbm, pairs_ref)
        ))
    ]
    for load in small:
        load.start()
    for a in range(4):
        for load in loads[a]:
            load.start()

    barrier = pltpu.get_barrier_semaphore()

    def greet(x, y):
        pl.semaphore_signal(barrier, inc=1, device_id=(x, y), device_id_type=MESH)

    for dx, dy in SIDES + CORNERS:
        @pl.when(exists(dx, dy))
        def _():
            greet(me_x + dx, me_y + dy)

    def group_xy(g):
        return 2 * (g // half_split) + my_x, 2 * lax.rem(g, half_split) + my_y

    @pl.loop(0, groups)
    def _(g):
        @pl.when(g != my_group)
        def _():
            x, y = group_xy(g)
            greet(x, y)

    lane = lax.broadcasted_iota(jnp.int32, (8, LANES), 1)
    row8 = lax.broadcasted_iota(jnp.int32, (8, LANES), 0)
    zero_tile = jnp.zeros((8, LANES), f32)

    for ref in (u_0, u_p):
        for x in (0, 1, nx + 2, nx + 3):
            ref[:, x] = jnp.zeros(ref.shape[:1] + ref.shape[2:], f32)

        @pl.loop(2, nx + 2)
        def _(x):
            for c in range(3):
                for h in range(halves):
                    ref[c, x, h, 0:8, :] = zero_tile
                    ref[c, x, h, ny + 8 : ny + 16, :] = zero_tile

    def shifted(parts, by):
        rows = parts[0].shape[0]
        lanes = lax.broadcasted_iota(jnp.int32, (rows, LANES), 1)
        rolled = [pltpu.roll(p, (-by) % LANES, axis=1) for p in parts]
        out = []
        n = len(parts)
        for h in range(n):
            other = (h + 1) % n if by > 0 else (h - 1) % n
            edge = lanes >= LANES - by if by > 0 else lanes < -by
            out.append(jnp.where(edge, rolled[other], rolled[h]))
        return out

    def put(c, x, rows, parts, shifts=True):
        for h, p in enumerate(parts):
            u_0[c, x, h, rows, :] = p
        if shifts:
            for h, p in enumerate(shifted(parts, 1)):
                u_p[c, x, h, rows, :] = p + 1.0 if c == 2 else p

    def zs(h):
        return slice(h * LANES, (h + 1) * LANES)

    def advance(s, x, t, speeds):
        rows = slice(8 * t, 8 * t + 8)
        for c in range(3):
            parts = []
            for h in range(halves):
                half = speeds[h][c]
                vel[c, x, rows, zs(h)] = half
                moved = dsp[c, x, rows, zs(h)] + dt * half
                dsp[c, x, rows, zs(h)] = moved
                if c == 0:
                    moved = moved + (x - mid_x).astype(f32)
                elif c == 1:
                    moved = moved + (row8 + (8 * t - mid_y)).astype(f32)
                parts.append(moved)
            put(c, x + 2, slice(8 + 8 * t, 16 + 8 * t), parts)
            for h, p in enumerate(shifted(parts, 2)):
                u_pp[c, x, h, rows, :] = p + 2.0 if c == 2 else p
            for h, p in enumerate(parts):
                for j in range(2):
                    if t == 0:
                        edges_y[s, 0, j, c, h, pl.ds(x, 1), :] = p[j : j + 1]
                    if t == tiles - 1:
                        edges_y[s, 1, j, c, h, pl.ds(x, 1), :] = p[7 - j : 8 - j]

    def near_layer(d):
        return 0 if d < 0 else nx - 1

    def copy_side(s, k, d, j):
        layer = near_layer(d) - d * j
        return pltpu.make_async_remote_copy(
            src_ref=u_0.at[:, 2 + layer, :, 8 : 8 + ny, :], dst_ref=got_x.at[s, k, j],
            send_sem=send_x.at[s, k, j], recv_sem=recv_x.at[s, k, j],
            device_id=(me_x + d, me_y), device_id_type=MESH,
        )

    def take_side(s, k, j):
        d = (-1, 1)[k]
        return pltpu.make_async_remote_copy(
            src_ref=got_x.at[s, k, j], dst_ref=got_x.at[s, k, j],
            send_sem=send_x.at[s, k, j], recv_sem=recv_x.at[s, k, j],
            device_id=(me_x + d, me_y), device_id_type=MESH,
        )

    def copy_edge(s, k, d, j):
        return pltpu.make_async_remote_copy(
            src_ref=edges_y.at[s, 1 - k, j], dst_ref=got_y.at[s, k, j],
            send_sem=send_y.at[s, k, j], recv_sem=recv_y.at[s, k, j],
            device_id=(me_x, me_y + d), device_id_type=MESH,
        )

    def take_edge(s, k, d, j):
        return pltpu.make_async_remote_copy(
            src_ref=got_y.at[s, k, j], dst_ref=got_y.at[s, k, j], send_sem=send_y.at[s, k, j],
            recv_sem=recv_y.at[s, k, j], device_id=(me_x, me_y + d), device_id_type=MESH,
        )

    def copy_corner(s, k, dx, dy):
        return pltpu.make_async_remote_copy(
            src_ref=edges_c.at[s, k], dst_ref=got_c.at[s, k], send_sem=send_c.at[s, k],
            recv_sem=recv_c.at[s, k], device_id=(me_x + dx, me_y + dy), device_id_type=MESH,
        )

    def take_corner(s, j, dx, dy):
        return pltpu.make_async_remote_copy(
            src_ref=got_c.at[s, j], dst_ref=got_c.at[s, j], send_sem=send_c.at[s, j],
            recv_sem=recv_c.at[s, j], device_id=(me_x + dx, me_y + dy), device_id_type=MESH,
        )

    partners = ((0, 1), (1, 0), (1, 1))

    def flipped(fx, fy):
        return my_x + (1 - 2 * my_x) * fx, my_y + (1 - 2 * my_y) * fy

    def copy_part(s, p, fx, fy):
        ix, iy = flipped(fx, fy)
        return pltpu.make_async_remote_copy(
            src_ref=part_send.at[s], dst_ref=part_got.at[s, my_id], send_sem=send_p.at[s, p],
            recv_sem=recv_p.at[s, p], device_id=(me_x + ix - my_x, me_y + iy - my_y),
            device_id_type=MESH,
        )

    def take_part(s, p, fx, fy):
        ix, iy = flipped(fx, fy)
        return pltpu.make_async_remote_copy(
            src_ref=part_send.at[s], dst_ref=part_got.at[s, ix * 2 + iy], send_sem=send_p.at[s, p],
            recv_sem=recv_p.at[s, p], device_id=(me_x + ix - my_x, me_y + iy - my_y),
            device_id_type=MESH,
        )

    def copy_group(i, g):
        x, y = group_xy(g)
        return pltpu.make_async_remote_copy(
            src_ref=fin.at[i], dst_ref=gathered.at[i, my_group], send_sem=send_g.at[i, g],
            recv_sem=recv_g.at[i, my_group], device_id=(x, y), device_id_type=MESH,
        )

    def take_group(i, g):
        x, y = group_xy(g)
        return pltpu.make_async_remote_copy(
            src_ref=fin.at[i], dst_ref=gathered.at[i, g], send_sem=send_g.at[i, g],
            recv_sem=recv_g.at[i, g], device_id=(x, y), device_id_type=MESH,
        )

    def share(i, rows):
        fin[i] = rows
        gathered[i, my_group] = rows

        @pl.loop(0, groups)
        def _(g):
            @pl.when(g != my_group)
            def _():
                copy_group(i, g).start()

    def length(m, own, x, h, y):
        dx, dy, dz = HALF[m]
        if dz == 2:
            near = [u_pp[c, x - 2, h, pl.ds(y - 8, 8), :] for c in range(3)]
        else:
            ref = u_p if dz else u_0
            near = [ref[c, x + dx, h, pl.ds(y + dy, 8), :] for c in range(3)]
        d = [near[c] - own[c] for c in range(3)]
        q = d[0] * d[0] + d[1] * d[1] + d[2] * d[2]
        rr[m, x, pl.ds(h * (ny + 16) + y, 8), :] = (
            q * lax.rsqrt(jnp.maximum(q, tiny)) - math.sqrt(square(HALF[m]))
        )

    def lengths(ms, x, h, y):
        own = [u_0[c, x, h, pl.ds(y, 8), :] for c in range(3)]
        for m in ms:
            length(m, own, x, h, y)

    every = list(range(PAIRS))
    dx_up = [m for m in every if HALF[m][0] == 1]
    dx_down = [m for m in every if HALF[m][0] == -1]
    x_two = INDEX[(2, 0, 0)]
    y_two = INDEX[(0, 2, 0)]
    dy_up = [m for m in every if HALF[m][1] == 1]
    dy_down = [m for m in every if HALF[m][1] < 0]

    def layer_lengths(x):
        for h in range(halves):
            for t in range(tiles):
                lengths(every, x + 2, h, 8 + 8 * t)

    ahead, behind_loop = 1, 3

    def inner_lengths():
        @pl.loop(ahead + behind_loop, nx, unroll=2)
        def _(x):
            layer_lengths(x)

    def side_lengths(base):
        for h in range(halves):
            for t in range(tiles):
                y = 8 + 8 * t
                lengths(dx_up, base + 1, h, y)
                lengths(dx_down, base + 2, h, y)

    def far_lengths(base):
        for h in range(halves):
            for t in range(tiles):
                lengths([x_two], base, h, 8 + 8 * t)
                lengths([x_two], base + 1, h, 8 + 8 * t)

    def edge_lengths():
        def one(ups, downs, x):
            for h in range(halves):
                for base in (0, ny):
                    if ups:
                        lengths(ups, x, h, base)
                    if downs:
                        lengths(downs, x, h, base + 8)

        @pl.loop(0, nx, unroll=2)
        def _(x):
            one(dy_up, dy_down, x + 2)

        one([m for m in dy_up if m in dx_up], [m for m in dy_down if m in dx_up], 1)
        one([m for m in dy_up if m in dx_down], [m for m in dy_down if m in dx_down], nx + 2)

    def plane_sums(c):
        sx = [c[i][0] + c[i][1] + c[i][2] for i in range(3)]
        fy = (c[0][2] + c[1][2] + c[2][2]) - (c[0][0] + c[1][0] + c[2][0])
        return [sx[2] - sx[0], fy, sx[0] + sx[1] + sx[2]]

    def forces(x, t):
        y = 8 + 8 * t
        rows = slice(8 * t, 8 * t + 8)
        total, back, back_two = [], [], []
        for h in range(halves):
            def forth(e):
                m = INDEX[e]
                at = h * (ny + 16) + y
                return rr[m, x + 2, at : at + 8, :] * factors[x, h, t, m]

            def behind(e):
                m = INDEX[e]
                at = h * (ny + 16) + y - e[1]
                return rr[m, x + 2 - e[0], at : at + 8, :] * factors[x, h, t, PAIRS + m]

            up = plane_sums([[forth((dx, dy, 1)) for dy in (-1, 0, 1)] for dx in (-1, 0, 1)])
            down = plane_sums([[behind((dx, dy, 1)) for dy in (-1, 0, 1)] for dx in (-1, 0, 1)])

            def net(e):
                return forth(e) - behind(e)

            a, b = net((1, 1, 0)), net((1, -1, 0))
            fx = (a + b) + (net((1, 0, 0)) + net((2, 0, 0)))
            fy = (a - b) + (net((0, 1, 0)) + net((0, 2, 0)))
            total.append([up[0] + fx, up[1] + fy, up[2] + forth((0, 0, 2))])
            back.append(down)
            back_two.append(behind((0, 0, 2)))
        for c in range(3):
            for h, p in enumerate(shifted([back[h][c] for h in range(halves)], -1)):
                total[h][c] = total[h][c] - p
        for h, p in enumerate(shifted(back_two, -2)):
            total[h][2] = total[h][2] - p
        for c in range(3):
            total[top][c] = total[top][c] + pf[c, x, rows, :]
        return total

    wide_lane = lax.broadcasted_iota(jnp.int32, (LANES, LANES), 1).astype(f32)
    wide_row = lax.broadcasted_iota(jnp.int32, (LANES, LANES), 0).astype(f32)
    r16 = lax.broadcasted_iota(jnp.int32, (ROWS, LANES), 0)

    def padded(a):
        n = a.shape[0]
        return a if n == LANES else jnp.concatenate([a, jnp.zeros((LANES - n, LANES), f32)], axis=0)

    def column(row):
        return jnp.broadcast_to(row, (LANES, LANES)).T

    def build_tables():
        for load in small:
            load.wait()
        where = []
        for c, (size, most) in enumerate(((2 * nx, slabs // 2), (2 * ny, half_split))):
            sums = jnp.sum(padded(qpos_ref[c]).T, axis=0, keepdims=True)
            cell = jnp.floor((sums * (1.0 / PTS) + 0.5) * (1.0 / size))
            where.append(jnp.clip(cell, 0.0, float(most - 1)))
        group = where[0] * float(half_split) + where[1]
        same = (column(group) == group) & (wide_row < wide_lane)
        rank = jnp.sum(jnp.where(same, 1.0, 0.0), axis=0, keepdims=True)
        place = group * float(ROWS) + jnp.minimum(rank, float(per_group - 1))
        place = jnp.where(wide_lane[0:1] < float(blocks), place, -1e6)
        place_col[...] = column(place)
        first = (my_group * ROWS).astype(f32)
        wide_place = jnp.broadcast_to(place, (ROWS, LANES))
        of_slot = jnp.where(wide_place == first + (r16 // per_block).astype(f32), 1.0, 0.0)
        of_state = jnp.where(
            wide_place == first + lax.rem(r16, per_group).astype(f32), 1.0, 0.0
        )

        def mine(ref):
            out = jnp.zeros((ROWS, LANES), f32)
            for c in range(3):
                out = jnp.where(r16 // per_group == c, exact_dot(of_state, padded(ref[c])), out)
            return out

        half = mine(qvel_ref) + 0.5 * dt * mine(qacc_ref)
        qv[...] = half
        qp[...] = mine(qpos_ref) + dt * half

        pairs_s[...] = jnp.full(pairs_s.shape, -1, jnp.int32)
        for s in range(subs):
            pairs_s[2 * s : 2 * s + 2, 0:slots] = pairs_ref[s]
        earlier = jnp.where(wide_row < wide_lane, 1.0, 0.0)
        for s in range(subs):
            target = pairs_s[2 * s : 2 * s + 1].astype(f32)
            chosen = pairs_s[2 * s + 1 : 2 * s + 2].astype(f32)
            hit = exact_dot(of_slot, jnp.where(wide_row == chosen, 1.0, 0.0))
            order = exact_dot(hit, earlier)
            hit = jnp.where(order == lax.rem(r16, per_block).astype(f32), hit, 0.0)
            table = exact_dot(hit, jnp.where(column(target) * float(SL) == wide_lane, 1.0, 0.0))
            onehot[s] = table
            onehot_t[s] = padded(table).T[0 : SL * nx]
            live = jnp.sum(table, axis=1, keepdims=True)
            penalty[s] = jnp.broadcast_to(far * (1.0 - live), (ROWS, LANES))

    build_tables()
    three = wide_row < float(3 * ROWS)
    of_row = wide_row - float(ROWS) * jnp.floor(wide_row * (1.0 / ROWS))
    for i in range(3 * per_group):
        spread_row[i] = jnp.where(three & (of_row == float(i)), 1.0, 0.0).astype(bf16)
        one = jnp.where(wide_lane == float(i), 1.0, 0.0).astype(bf16)
        sum_column[i] = jnp.concatenate([one, one], axis=0)

    for a in range(3):
        for load in loads[a]:
            load.wait()

    def inside(visit):
        @pl.loop(2, nx - 2, unroll=4)
        def _(x):
            for t in range(1, tiles - 1):
                visit(x, t)

    def sweep(visit, after_edges, after_sides, after_layer, whole=False):
        @pl.loop(0, nx, unroll=4)
        def _(x):
            for t in (0, tiles - 1):
                visit(x, t)

        after_edges()

        @pl.loop(0, 2, unroll=2)
        def _(i):
            for t in range(1, tiles - 1):
                visit(i * (nx - 1), t)
            after_layer(i * (nx - 1))

        after_sides()

        if whole:
            inside(visit)
        @pl.loop(0, 2, unroll=2)
        def _(i):
            for t in range(1, tiles - 1):
                visit(1 + i * (nx - 3), t)

        @pl.loop(1, nx - 1)
        def _(x):
            after_layer(x)

    def send_edges(s):
        for k, (dx, dy) in enumerate(CORNERS):
            x = 2 if dx < 0 else nx + 1
            y = 8 if dy < 0 else ny + 7
            for c in range(3):
                for h in range(halves):
                    edges_c[s, k, c, h] = u_0[c, x, h, y : y + 1, :]
        for k, d in enumerate((1, -1)):
            @pl.when(exists(0, d))
            def _():
                copy_edge(s, k, d, 0).start()
        for k, (dx, dy) in enumerate(CORNERS):
            @pl.when(exists(dx, dy))
            def _():
                copy_corner(s, k, dx, dy).start()

    def send_far(s):
        send_sides(s, 1)
        for k, d in enumerate((1, -1)):
            @pl.when(exists(0, d))
            def _():
                copy_edge(s, k, d, 1).start()

    def send_sides(s, j):
        for k, d in enumerate((1, -1)):
            @pl.when(exists(d, 0))
            def _():
                copy_side(s, k, d, j).start()

    def nothing(*args):
        pass

    def first_step(x, t):
        rows = slice(8 * t, 8 * t + 8)
        advance(0, x, t, [
            [vel[c, x, rows, zs(h)] + 0.5 * dt * acc[c, x, rows, zs(h)] for c in range(3)]
            for h in range(halves)
        ])

    def greeted():
        count = groups - 1
        for dx, dy in SIDES + CORNERS:
            count = count + jnp.where(exists(dx, dy), 1, 0)
        pl.semaphore_wait(barrier, count)
        send_edges(0)

    sweep(first_step, greeted, lambda: send_sides(0, 0), nothing, True)
    send_far(0)

    def build_factors():
        above = [
            (word_bits(lambda e: e[i] == -1), word_bits(lambda e: e[i] == -2),
             word_bits(lambda e: e[i] == 1), word_bits(lambda e: e[i] == 2))
            for i in range(3)
        ]

        def allowed(at, size, i, w):
            one_down, two_down, one_up, two_up = (bits[w] for bits in above[i])
            keep = jnp.where(at < 1, 255 & ~one_down, 255)
            keep = keep & jnp.where(at < 2, 255 & ~two_down, 255)
            keep = keep & jnp.where(at > size - 2, 255 & ~one_up, 255)
            return keep & jnp.where(at > size - 3, 255 & ~two_up, 255)

        for h in range(halves):
            for t in range(tiles):
                for w in range(4):
                    at_y = me_y * ny + t * 8 + row8
                    at_z = lane + h * LANES
                    valid[h, t, w] = allowed(at_y, splits * ny, 1, w) & allowed(at_z, nz, 2, w)

        for load in loads[3]:
            load.wait()

        @pl.loop(0, nx, unroll=2)
        def _(x):
            ok_x = [allowed(me_x * nx + x, slabs * nx, 0, w) for w in range(4)]
            for t in range(tiles):
                rows = slice(8 * t, 8 * t + 8)
                words = [
                    [mask_ref[w, x, rows, zs(h)] & (valid[h, t, w] & ok_x[w]) for w in range(4)]
                    for h in range(halves)
                ]
                moved = {0: words}
                for by in (1, 2):
                    cols = [shifted([words[h][w] for h in range(halves)], by) for w in range(4)]
                    moved[by] = [[cols[w][h] for w in range(4)] for h in range(halves)]
                for h in range(halves):
                    for m, e in enumerate(HALF):
                        scale = bond_stiffness / square(e) * (2.0 if square(e) == 4 else 1.0)
                        minus = (-e[0], -e[1], -e[2])
                        for at, bond, frame in ((m, e, 0), (PAIRS + m, minus, e[2])):
                            n = NUMBER[bond]
                            bit = moved[frame][h][n // 8] & (1 << (n % 8))
                            factors[x, h, t, at] = jnp.where(bit != 0, scale, 0.0)

    stretch = math.sqrt(1.0 / (math.log(2.0) * contact_width))
    strength = contact_stiffness / stretch

    def contact(s):
        base = jnp.where(
            r16 // per_group == 0, (me_x * nx + mid_x).astype(f32),
            jnp.where(r16 // per_group == 1, (me_y * ny + mid_y).astype(f32), float(nz - SL)),
        )
        rel = (qp[...] - base) * stretch
        hi = rel.astype(bf16).astype(f32)
        mid = (rel - hi).astype(bf16).astype(f32)
        low = (rel - hi - mid).astype(bf16).astype(f32)
        split = padded(jnp.concatenate([hi, mid, low], axis=0)).T.astype(bf16)
        for i in range(3 * per_group):
            qb[i] = plain_dot(split, spread_row[i])
        for c in range(3):
            cols = []
            for t in range(tiles):
                col = zero_tile
                for x in range(nx):
                    tile = u_0[c, x + 2, top, 8 + 8 * t : 16 + 8 * t, :]
                    tile = pltpu.roll(tile, SL * x + SL, axis=1)
                    col = jnp.where(lane // SL == x, tile, col)
                cols.append(col)
            stack = []
            for z in range(SL):
                for col in cols:
                    col = pltpu.roll(col, (LANES - z) % LANES, axis=1) if z else col
                    stack.append(col + float(z) if c == 2 else col)
            places = jnp.concatenate(stack, axis=0).T[0 : SL * nx] * stretch
            table = exact_dot(onehot[s, :, 0 : SL * nx], places)
            psel[c] = table + penalty[s] if c == 0 else table
        for x in range(ahead):
            layer_lengths(x)

        @pl.loop(0, per_group)
        def _(r):
            first = r * per_block
            points = [
                [jnp.broadcast_to(psel[c, pl.ds(first + j, 1), :], (8, LANES)) for c in range(3)]
                for j in range(per_block)
            ]
            on_points = [[zero_tile] * 3 for _ in range(per_block)]
            for i in range(PTS // 8):
                rows = slice(8 * i, 8 * i + 8)
                q = [qb[c * per_group + r, rows, :] for c in range(3)]
                pulls = [None] * 3
                for j in range(per_block):
                    d = [points[j][c] - q[c] for c in range(3)]
                    w = jnp.exp2(-(d[0] * d[0] + d[1] * d[1] + d[2] * d[2]))
                    for c in range(3):
                        pull = w * d[c]
                        pulls[c] = pull if pulls[c] is None else pulls[c] + pull
                        on_points[j][c] = on_points[j][c] + pull
                for c in range(3):
                    qb[c * per_group + r, rows, :] = pulls[c]
            for j in range(per_block):
                for c in range(3):
                    slot_rows[c, pl.ds(first + j, 1), :] = strength * jnp.sum(
                        on_points[j][c], axis=0, keepdims=True
                    )

        total = None
        for i in range(3 * per_group):
            hi = qb[i].astype(bf16)
            low = (qb[i] - hi.astype(f32)).astype(bf16)
            part = plain_dot(jnp.concatenate([hi, low], axis=1), sum_column[i])
            total = part if total is None else total + part
        rows = -strength * total.T[0:ROWS]
        part_send[s] = rows
        part_got[s, my_id] = rows
        for c in range(3):
            spread = padded(exact_dot(onehot_t[s], slot_rows[c])).T
            for t in range(tiles):
                packed = zero_tile
                for z in range(SL):
                    tile = spread[z * ny + 8 * t : z * ny + 8 * t + 8]
                    tile = pltpu.roll(tile, z, axis=1) if z else tile
                    packed = jnp.where(lax.rem(lane, SL) == z, tile, packed)
                for x in range(nx):
                    tile = pltpu.roll(packed, LANES - SL - SL * x, axis=1) if x < nx else packed
                    pf[c, x, 8 * t : 8 * t + 8, :] = jnp.where(lane >= LANES - SL, tile, 0.0)
        for x in range(ahead, ahead + behind_loop):
            layer_lengths(x)
        for p, (fx, fy) in enumerate(partners):
            copy_part(s, p, fx, fy).start()

    def particle_force(s):
        for p, (fx, fy) in enumerate(partners):
            take_part(s, p, fx, fy).wait()
        total = part_got[s, 0] + part_got[s, 1] + part_got[s, 2] + part_got[s, 3]
        return inverse_mass * total

    slot_rows[...] = jnp.zeros(slot_rows.shape, f32)

    def put_side(s, k, j):
        d = (-1, 1)[k]
        x = 1 - j if d < 0 else nx + 2 + j
        for c in range(3):
            parts = [got_x[s, k, j, c, h] for h in range(halves)]
            if c == 0:
                parts = [p + float(d * nx) for p in parts]
            put(c, x, slice(8, 8 + ny), parts, j == 0)

    def put_corner(s, dx, dy):
        j = CORNERS.index((-dx, -dy))
        take_corner(s, j, dx, dy).wait_recv()
        x = 1 if dx < 0 else nx + 2
        y = 7 if dy < 0 else ny + 8
        for c in range(3):
            parts = [got_c[s, j, c, h] for h in range(halves)]
            if c == 0:
                parts = [p + float(dx * nx) for p in parts]
            if c == 1:
                parts = [p + float(dy * ny) for p in parts]
            put(c, x, slice(y, y + 1), parts)

    def put_edge(s, k, d, j):
        take_edge(s, k, d, j).wait_recv()
        y = 7 - j if d < 0 else ny + 8 + j
        for c in range(3):
            parts = [got_y[s, k, j, c, h] for h in range(halves)]
            if c == 1:
                parts = [p + float(d * ny) for p in parts]
            moved = shifted(parts, 1) if j == 0 else []
            if c == 2:
                moved = [p + 1.0 for p in moved]
            for ref, values in ((u_0, parts), (u_p, moved)):
                for h, p in enumerate(values):
                    for x in range(nx):
                        ref[c, x + 2, h, y : y + 1, :] = p[x : x + 1]

    def sent(s):
        for k, d in enumerate((1, -1)):
            @pl.when(exists(d, 0))
            def _():
                for j in range(2):
                    copy_side(s, k, d, j).wait_send()

            @pl.when(exists(0, d))
            def _():
                for j in range(2):
                    copy_edge(s, k, d, j).wait_send()
        for k, (dx, dy) in enumerate(CORNERS):
            @pl.when(exists(dx, dy))
            def _():
                copy_corner(s, k, dx, dy).wait_send()

    def substep(s):
        last = s == subs - 1

        @pl.when(s > 0)
        def _():
            half = qv[...] + dt * particle_force(s - 1)
            qv[...] = half
            qp[...] = qp[...] + dt * half

        @pl.when(last)
        def _():
            share(0, qp[...])
            for c in range(3):
                pltpu.make_async_copy(dsp.at[c, 0:nx, 0:ny], disp_out.at[c], out_sem.at[0, c]).start()

        contact(s)
        inner_lengths()

        @pl.when(s == 0)
        def _():
            build_factors()

        def step(x, t):
            rows = slice(8 * t, 8 * t + 8)
            total = forces(x, t)
            advance(s + 1, x, t, [
                [vel[c, x, rows, zs(h)] + dt * total[h][c] for c in range(3)]
                for h in range(halves)
            ])

        def finish_speed(x, t):
            rows = slice(8 * t, 8 * t + 8)
            total = forces(x, t)
            for h in range(halves):
                for c in range(3):
                    vel[c, x, rows, zs(h)] = vel[c, x, rows, zs(h)] + 0.5 * dt * total[h][c]

        @pl.when(s < subs - 1)
        def _():
            inside(step)

        @pl.when(last)
        def _():
            inside(finish_speed)

        for k, d in enumerate((-1, 1)):
            @pl.when(exists(d, 0))
            def _():
                take_side(s, k, 0).wait_recv()
                put_side(s, k, 0)
        for dx, dy in CORNERS:
            @pl.when(exists(dx, dy))
            def _():
                put_corner(s, dx, dy)
        for k, d in enumerate((-1, 1)):
            @pl.when(exists(0, d))
            def _():
                put_edge(s, k, d, 0)

        @pl.loop(0, 2)
        def _(i):
            side_lengths(i * nx)

        edge_lengths()

        @pl.when(last)
        def _():
            share(1, qv[...] + 0.5 * dt * particle_force(s))

        for k, d in enumerate((-1, 1)):
            @pl.when(exists(d, 0))
            def _():
                take_side(s, k, 1).wait_recv()
                put_side(s, k, 1)

            @pl.when(exists(0, d))
            def _():
                put_edge(s, k, d, 1)

        @pl.loop(0, 2)
        def _(i):
            far_lengths(i * nx)

        @pl.loop(0, nx, unroll=2)
        def _(x):
            for h in range(halves):
                for base in (0, ny):
                    lengths([y_two], x + 2, h, base)

        sent(s)

        @pl.when(s < subs - 1)
        def _():
            sweep(step, lambda: send_edges(s + 1), lambda: send_sides(s + 1, 0), nothing)
            send_far(s + 1)

        @pl.when(last)
        def _():
            def leave(x):
                pltpu.make_async_copy(vel.at[:, x, 0:ny], vel_out.at[:, x], out_sem.at[1, x]).start()

            sweep(finish_speed, nothing, nothing, leave)

    @pl.loop(0, subs)
    def _(s):
        substep(s)

    where = place_col[0:blocks]
    for i, dst in enumerate((pos_out, pvel_out)):
        @pl.loop(0, groups)
        def _(g):
            @pl.when(g != my_group)
            def _():
                take_group(i, g).wait()

        for c in range(3):
            out = None
            for k in range(0, groups * ROWS, LANES):
                rows = gathered[i, k // ROWS : (k + LANES) // ROWS].reshape(-1, LANES)
                pick = jnp.where(
                    where + float(c * per_group - k) == wide_lane[0:blocks], 1.0, 0.0
                )[:, 0 : rows.shape[0]]
                part = exact_dot(pick, rows)
                out = part if out is None else out + part
            ends[i, c] = out
        pltpu.make_async_copy(ends.at[i], dst, end_sem.at[i]).start()

    for c in range(3):
        pltpu.make_async_copy(dsp.at[c, 0:nx, 0:ny], disp_out.at[c], out_sem.at[0, c]).wait()

    @pl.loop(0, nx)
    def _(x):
        pltpu.make_async_copy(vel.at[:, x, 0:ny], vel_out.at[:, x], out_sem.at[1, x]).wait()

    for i, dst in enumerate((pos_out, pvel_out)):
        pltpu.make_async_copy(ends.at[i], dst, end_sem.at[i]).wait()


def finish_kernel(n, *refs):
    copies = [pltpu.make_async_copy(refs[i], refs[n + i], refs[-1].at[i]) for i in range(n)]
    for copy in copies:
        copy.start()
    for copy in copies:
        copy.wait()


def finish(*arrays):
    anywhere = pl.BlockSpec(memory_space=pl.ANY)
    n = len(arrays)
    return pl.pallas_call(
        functools.partial(finish_kernel, n),
        out_shape=tuple(jax.ShapeDtypeStruct(a.shape, a.dtype) for a in arrays),
        in_specs=[anywhere] * n,
        out_specs=(anywhere,) * n,
        scratch_shapes=[pltpu.SemaphoreType.DMA((n,))],
        compiler_params=pltpu.CompilerParams(vmem_limit_bytes=4 * 1024 * 1024),
    )(*arrays)


def per_device(
    slabs, splits,
    displacement, velocity, acceleration, bond_masks, proj_pos, proj_vel, proj_acc, contact_pairs
):
    _, nx, ny, nz = displacement.shape
    subs = contact_pairs.shape[0]
    blocks = proj_pos.shape[0]
    groups = (slabs // 2) * (splits // 2)
    per_group = blocks // groups
    halves = nz // LANES
    assert nx == SB_DEV and ny * SL == PTS and ny % 8 == 0
    assert per_group * 3 <= ROWS and blocks <= LANES and contact_pairs.shape[2] <= ROWS
    assert (groups * ROWS) % LANES == 0 or groups * ROWS < LANES

    dims = (subs, nx, ny, nz, slabs, splits, per_group, blocks)
    anywhere = pl.BlockSpec(memory_space=pl.ANY)
    padded = (3, nx + 5, halves, ny + 16, LANES)
    block = (3, nx + 1, ny + 8, nz)
    dma = pltpu.SemaphoreType.DMA
    scratch = [
        pltpu.VMEM((3, blocks, PTS), f32),
        pltpu.VMEM((3, blocks, PTS), f32),
        pltpu.VMEM((3, blocks, PTS), f32),
        pltpu.VMEM(contact_pairs.shape, jnp.int32),
        pltpu.VMEM((2, 3, blocks, PTS), f32),
        pltpu.VMEM(padded, f32),
        pltpu.VMEM(padded, f32),
        pltpu.VMEM((3, nx + 1, halves, ny + 8, LANES), f32),
        pltpu.VMEM(block, f32),
        pltpu.VMEM(block, f32),
        pltpu.VMEM(block, f32),
        pltpu.VMEM((4, nx, ny, nz), jnp.int32),
        pltpu.VMEM((halves, ny // 8, 4, 8, LANES), jnp.int32),
        pltpu.VMEM((nx, halves, ny // 8, 2 * PAIRS, 8, LANES), f32),
        pltpu.VMEM((PAIRS, nx + 3, halves * (ny + 16) + 8, LANES), f32),
        pltpu.VMEM((subs, 2, 2, 3, halves, nx, LANES), f32),
        pltpu.VMEM((subs, 4, 3, halves, 1, LANES), f32),
        pltpu.VMEM((subs, 2, 2, 3, halves, ny, LANES), f32),
        pltpu.VMEM((subs, 2, 2, 3, halves, nx, LANES), f32),
        pltpu.VMEM((subs, 4, 3, halves, 1, LANES), f32),
        pltpu.VMEM((3 * per_group, PTS, LANES), f32),
        pltpu.VMEM((3 * per_group, LANES, LANES), bf16),
        pltpu.VMEM((3 * per_group, 2 * LANES, LANES), bf16),
        pltpu.VMEM((3, ROWS, LANES), f32),
        pltpu.VMEM((3, LANES, LANES), f32),
        pltpu.VMEM((3, nx, ny, LANES), f32),
        pltpu.VMEM((8, LANES), jnp.int32),
        pltpu.VMEM((subs, ROWS, LANES), f32),
        pltpu.VMEM((subs, SL * nx, LANES), f32),
        pltpu.VMEM((subs, ROWS, LANES), f32),
        pltpu.VMEM((LANES, LANES), f32),
        pltpu.VMEM((ROWS, LANES), f32),
        pltpu.VMEM((ROWS, LANES), f32),
        pltpu.VMEM((subs, ROWS, LANES), f32),
        pltpu.VMEM((subs, 4, ROWS, LANES), f32),
        pltpu.VMEM((2, ROWS, LANES), f32),
        pltpu.VMEM((2, groups, ROWS, LANES), f32),
        dma((4, 2)), dma((4,)), dma((2, nx)), dma((2,)),
        dma((subs, 2, 2)), dma((subs, 2, 2)), dma((subs, 2, 2)), dma((subs, 2, 2)),
        dma((subs, 4)), dma((subs, 4)), dma((subs, 3)), dma((subs, 3)),
        dma((2, groups)), dma((2, groups)),
    ]
    moved, speed, points, point_speed = pl.pallas_call(
        functools.partial(kernel, dims),
        out_shape=(
            pltpu.VMEM(displacement.shape, f32),
            pltpu.VMEM(displacement.shape, f32),
            pltpu.VMEM((3, blocks, PTS), f32),
            pltpu.VMEM((3, blocks, PTS), f32),
        ),
        in_specs=[anywhere] * 8,
        out_specs=(anywhere,) * 4,
        scratch_shapes=scratch,
        compiler_params=pltpu.CompilerParams(
            collective_id=0, has_side_effects=True, vmem_limit_bytes=58 * 1024 * 1024
        ),
    )(
        displacement, velocity, acceleration, bond_masks,
        jnp.moveaxis(proj_pos, 1, 0), jnp.moveaxis(proj_vel, 1, 0), jnp.moveaxis(proj_acc, 1, 0),
        contact_pairs,
    )
    moved, speed, points, point_speed = finish(moved, speed, points, point_speed)
    return moved, speed, jnp.moveaxis(points, 0, 1), jnp.moveaxis(point_speed, 0, 1)


def solution(mesh):
    cells = P(None, "slab", "split", None)
    return jax.shard_map(
        functools.partial(per_device, mesh.shape["slab"], mesh.shape["split"]),
        mesh=mesh,
        in_specs=(cells, cells, cells, cells, P(), P(), P(), P(None, None, ("slab", "split"))),
        out_specs=(cells, cells, P(), P()),
        check_vma=False,
    )
```
